128 devices in a mesh: seq: 32 (over x_hi, z, y), tensor: 2 (over core), dp: 2 (over x_lo).
Axes of the slice: x: 4 (x_hi: 2, x_lo: 2; x = x_hi * 2 + x_lo), y: 4, z: 4, core: 2. Of those that a mesh axis runs over, the one named last changes fastest.
Arguments:
- inputs: bfloat16 [2, 24576, 1536], P('dp', 'seq', 'tensor'), may hold values from -6 to 6
- lengths: int32 [2], P('dp'), may hold values from 6144 to 24576, as said below
- cotangent: bfloat16 [2, 24576, 1536], P('dp', 'seq', 'tensor'), may hold values from -6 to 6
- w_value: bfloat16 [1536, 1536], P(None, 'tensor'), may hold values from -0.15625 to 0.15625
- w_gate: bfloat16 [1536, 1536], P(None, 'tensor'), may hold values from -0.15625 to 0.15625
- kernel: bfloat16 [31, 1536], P(None, 'tensor'), may hold values from -1 to 1
- w_out: bfloat16 [1536, 1536], P('tensor'), may hold values from -0.15625 to 0.15625
Outputs:
- output: bfloat16 [2, 24576, 1536], P('dp', 'seq', 'tensor')
- input_gradient: bfloat16 [2, 24576, 1536], P('dp', 'seq', 'tensor')
- value_grad: float32 [1536, 1536], P(('seq', 'dp'), 'tensor')
- gate_grad: float32 [1536, 1536], P(('seq', 'dp'), 'tensor')
- kernel_grad: float32 [31, 1536], P(None, 'tensor')
- out_grad: float32 [1536, 1536], P('tensor', ('seq', 'dp'))
The draws below stay inside these ranges and needn't reach their ends.
Inputs may be any that keep to these rules, and one draw needn't show every extreme that they name: `lengths`: in every draw some utterance has all 24576 frames valid.
All inputs are finite; a program needn't handle non-finite values.
Results may differ from the reference program's by a relative error of at most 0.009.
Values may be sent and summed in bfloat16 or wider, within the bound.
A program may use at most 128 MiB of HBM per device.

```python
import jax
import jax.numpy as jnp
from jax import lax

D = 1536
KERNEL = 31
LENGTH = 24576
UTTS = 2


def draw_lengths(key, part):
    first, second = jax.random.split(jax.random.fold_in(key, 17))
    drawn = jax.random.randint(first, (UTTS,), LENGTH // 4, LENGTH + 1, dtype=jnp.int32)
    chosen = jax.random.randint(second, (), 0, UTTS, dtype=jnp.int32)
    return jnp.where(jnp.arange(UTTS, dtype=jnp.int32) == chosen, jnp.int32(LENGTH), drawn)


def raised(values, rng, source, target, parts, factor):
    owner, partner = [(jnp.arange(values.shape[position]) // (values.shape[position] // parts)).reshape([-1 if axis == position else 1 for axis in range(values.ndim)]) for position in (source, target)]
    chosen = jax.random.permutation(rng, parts)[partner]
    strong = (owner == chosen) | (owner == (partner + parts // 2) % parts)
    return jnp.where(strong, factor * values, values)


def shard_levels(own_key, shape, cuts, least, top_value):
    def one(position, parts):
        heights = jax.random.uniform(jax.random.fold_in(jax.random.fold_in(own_key, 6), position), (parts,), jnp.float32, least / len(cuts), top_value / len(cuts))
        return jnp.repeat(jnp.exp(heights), shape[position] // parts).reshape((-1,) + (1,) * (len(shape) - position - 1))

    gain = one(*cuts[0])
    for cut in cuts[1:]:
        gain = gain * one(*cut)
    return gain


def noise(own_key, dims, deviation, limit, shards=(), held_as=jnp.bfloat16):
    values = deviation * jax.random.normal(own_key, dims, jnp.float32)
    if shards:
        values = values * shard_levels(own_key, dims, shards, -0.22, 0.18)
    return jnp.clip(values, -limit, limit).astype(held_as)


def bell_draw_with(own_key, extent, width, limit, shards, heavy, kind=jnp.bfloat16):
    result = width * jax.random.normal(own_key, extent, jnp.float32)
    if shards:
        result = result * shard_levels(own_key, extent, shards, -0.22, 0.18)
    return jnp.clip(raised(result, jax.random.fold_in(own_key, 3), *heavy), -limit, limit).astype(kind)


def setup_inputs(seed: int = 0) -> dict:
    streams_of = jax.random.split(jax.random.key(seed), 8)
    inputs = bell_draw_with(streams_of[0], (UTTS, LENGTH, D), 1.0, 6.0, ((0, 2), (1, 32), (2, 2)), (1, 2, 32, 2.75))
    lengths = draw_lengths(jax.random.fold_in(streams_of[7], 71), 0)
    cotangent = bell_draw_with(streams_of[2], (UTTS, LENGTH, D), 1.0, 6.0, ((0, 2), (1, 32), (2, 2)), (1, 2, 32, 2.75))
    w_value = noise(streams_of[3], (D, D), D ** -0.5, 0.15625, ((1, 2),))
    w_gate = noise(streams_of[4], (D, D), D ** -0.5, 0.15625, ((1, 2),))
    kernel = noise(streams_of[5], (KERNEL, D), KERNEL ** -0.5, 1.0, ((1, 2),))
    w_out = noise(streams_of[6], (D, D), D ** -0.5, 0.15625, ((0, 2),))
    return dict(inputs=inputs, lengths=lengths, cotangent=cotangent, w_value=w_value, w_gate=w_gate, kernel=kernel, w_out=w_out)


epsilon = 1e-05

def layer_normalizer(values):
    center = values - lax.optimization_barrier(jnp.mean(values, axis=-1, keepdims=True))
    inverse = lax.rsqrt(lax.optimization_barrier(jnp.mean(center * center, axis=-1, keepdims=True)) + epsilon)
    return (center * inverse, inverse)

def utterance(frame_total, length, cotangent, w_value, w_gate, kernel, w_out):
    count = frame_total.shape[0]
    half = (KERNEL - 1) // 2
    valid = (jnp.arange(count, dtype=jnp.int32) < length).astype(jnp.float32)[:, None]
    taps = kernel.astype(jnp.float32)
    centered_scaled, inverse_deviation_one = layer_normalizer(frame_total.astype(jnp.float32))
    normalized_rows = centered_scaled.astype(jnp.bfloat16)
    values = jnp.dot(normalized_rows, w_value, preferred_element_type=jnp.float32)
    gates = jnp.dot(normalized_rows, w_gate, preferred_element_type=jnp.float32)
    sigma = jax.nn.sigmoid(gates)
    hidden = (values * sigma * valid).astype(jnp.bfloat16)
    padded = jnp.pad(hidden, ((half, half), (0, 0))).astype(jnp.float32)
    conv = jnp.zeros((count, hidden.shape[1]), jnp.float32)
    for offset in range(KERNEL):
        conv = conv + padded[offset:offset + count] * taps[offset]
    zhat, rstd_two = layer_normalizer(conv)
    swish_gate = jax.nn.sigmoid(zhat)
    swished = (zhat * swish_gate).astype(jnp.bfloat16)
    output = (frame_total.astype(jnp.float32) + jnp.dot(swished, w_out, preferred_element_type=jnp.float32)).astype(jnp.bfloat16)
    out_grad = jnp.dot(swished.T, cotangent, preferred_element_type=jnp.float32)
    dswish = jnp.dot(cotangent, w_out.T, preferred_element_type=jnp.float32)
    dswish = dswish * (swish_gate + zhat * swish_gate * (1.0 - swish_gate))
    dconv = rstd_two * (dswish - lax.optimization_barrier(jnp.mean(dswish, axis=-1, keepdims=True)) - zhat * lax.optimization_barrier(jnp.mean(dswish * zhat, axis=-1, keepdims=True)))
    dconv = dconv.astype(jnp.bfloat16)
    slope = dconv.astype(jnp.float32)
    kernel_grad = jnp.stack([lax.optimization_barrier(jnp.sum(padded[offset:offset + count] * slope, axis=0)) for offset in range(KERNEL)])
    slope_pad = jnp.pad(slope, ((half, half), (0, 0)))
    dhidden = jnp.zeros((count, hidden.shape[1]), jnp.float32)
    for offset in range(KERNEL):
        dhidden = dhidden + slope_pad[2 * half - offset:2 * half - offset + count] * taps[offset]
    dhidden = dhidden * valid
    dvalues = (dhidden * sigma).astype(jnp.bfloat16)
    dgates = (dhidden * values * sigma * (1.0 - sigma)).astype(jnp.bfloat16)
    value_grad = jnp.dot(normalized_rows.T, dvalues, preferred_element_type=jnp.float32)
    gate_grad = jnp.dot(normalized_rows.T, dgates, preferred_element_type=jnp.float32)
    normalized_grad = jnp.dot(dvalues, w_value.T, preferred_element_type=jnp.float32) + jnp.dot(dgates, w_gate.T, preferred_element_type=jnp.float32)
    input_gradient = cotangent.astype(jnp.float32) + inverse_deviation_one * (normalized_grad - lax.optimization_barrier(jnp.mean(normalized_grad, axis=-1, keepdims=True)) - centered_scaled * lax.optimization_barrier(jnp.mean(normalized_grad * centered_scaled, axis=-1, keepdims=True)))
    return (output, input_gradient.astype(jnp.bfloat16), value_grad, gate_grad, kernel_grad, out_grad)

def reference(inputs, lengths, cotangent, w_value, w_gate, kernel, w_out):

    def single(packed):
        return utterance(packed[0], packed[1], packed[2], w_value, w_gate, kernel, w_out)
    output, input_gradient, value_grad, gate_grad, kernel_grad, out_grad = lax.map(single, (inputs, lengths, cotangent))
    return (output, input_gradient, lax.optimization_barrier(jnp.sum(value_grad, axis=0)), lax.optimization_barrier(jnp.sum(gate_grad, axis=0)), lax.optimization_barrier(jnp.sum(kernel_grad, axis=0)), lax.optimization_barrier(jnp.sum(out_grad, axis=0)))
```

```python
import functools

import jax
import jax.numpy as jnp
from jax import lax
from jax.experimental import pallas as pl
from jax.experimental.pallas import tpu as pltpu
from jax.sharding import PartitionSpec as P

epsilon = 1e-05
MESH = pl.DeviceIdType.MESH
BF16, F32 = jnp.bfloat16, jnp.float32
ORDERS = ("xyz", "yzx", "zxy")
GRADS = 3
LEFT = {
    "xyz": ((4, 4), (4,), ()),
    "yzx": ((2, 4, 2), (2, 2), ()),
    "zxy": ((2, 4, 2), (4,), ()),
}


class Torus:
    def __init__(self):
        seq, low = lax.axis_index("seq"), lax.axis_index("dp")
        self.at = {
            "x": lax.div(seq, 16) * 2 + low,
            "y": lax.rem(seq, 4),
            "z": lax.rem(lax.div(seq, 4), 4),
        }

    def moved(self, axis, by):
        return lax.rem(self.at[axis] + (by + 4), 4)

    def peer(self, axis, by):
        at = dict(self.at)
        at[axis] = self.moved(axis, by)
        return {
            "seq": (lax.div(at["x"], 2) * 4 + at["z"]) * 4 + at["y"],
            "dp": lax.rem(at["x"], 2),
        }


def part_of(order, phase, coord):
    every = slice(None)
    high, low = lax.div(coord, 2), lax.rem(coord, 2)
    if phase == 0:
        return {
            "x": (high, every, every, low),
            "y": (every, every, coord, every),
            "z": (every, coord, every, every),
        }[order[0]]
    if phase == 1:
        return {"xyz": (every, coord), "yzx": (every, coord, every), "zxy": (high, every, low)}[order]
    return {"xyz": (coord,), "yzx": (high, low), "zxy": (coord,)}[order]


def greet(torus):
    barrier = pltpu.get_barrier_semaphore()
    for axis in "xyz":
        for by in (1, 2, 3):
            pl.semaphore_signal(
                barrier, inc=1, device_id=torus.peer(axis, by), device_id_type=MESH
            )
    pl.semaphore_wait(barrier, 9)


class Scatter:
    def __init__(self, torus, grad, strip, source, landed, sums, out, send, recv):
        self.torus, self.grad, self.strip = torus, grad, strip
        self.source, self.landed, self.sums, self.out = source, landed, sums, out
        self.send, self.recv = send, recv
        self.order = ORDERS[strip // 2]
        self.way = 1 if strip % 2 == 0 else -1

    def held(self, phase, coord):
        part = part_of(self.order, phase, coord)
        if phase == 0:
            return self.source.at[(self.grad, self.strip) + part]
        return self.sums[self.strip // 2][phase - 1].at[(self.grad, self.strip % 2) + part]

    def slot(self, phase, which):
        return self.landed[self.strip // 2][phase].at[self.grad, self.strip % 2, which]

    def copy(self, phase, which, ref, by):
        number = ((self.grad * 6 + self.strip) * 3 + phase) * 3 + which
        return pltpu.make_async_remote_copy(
            src_ref=ref,
            dst_ref=self.slot(phase, which),
            send_sem=self.send.at[number],
            recv_sem=self.recv.at[number],
            device_id=self.torus.peer(self.order[phase], by),
            device_id_type=MESH,
        )

    def place(self, phase, by):
        return self.torus.moved(self.order[phase], by)

    def through(self, phase):
        return self.copy(phase, 0, self.held(phase, self.place(phase, 2)), self.way)

    def straight(self, phase):
        return self.copy(phase, 1, self.held(phase, self.place(phase, -self.way)), -self.way)

    def onward(self, phase):
        return self.copy(phase, 2, self.slot(phase, 0), self.way)

    def begin(self, phase):
        self.through(phase).start()
        self.straight(phase).start()

    def relay(self, phase):
        self.through(phase).wait_recv()
        slot = self.slot(phase, 0)
        mine = self.held(phase, self.place(phase, self.way))
        slot[...] = (slot[...].astype(F32) + mine[...].astype(F32)).astype(BF16)
        self.onward(phase).start()

    def finish(self, phase):
        self.straight(phase).wait_recv()
        self.onward(phase).wait_recv()
        mine = self.held(phase, self.torus.at[self.order[phase]])
        total = (
            mine[...].astype(F32)
            + self.slot(phase, 1)[...].astype(F32)
            + self.slot(phase, 2)[...].astype(F32)
        )
        if phase < 2:
            self.sums[self.strip // 2][phase][self.grad, self.strip % 2] = total.astype(BF16)
        else:
            self.out[self.grad, :, 128 * self.strip : 128 * self.strip + 128] = total

    def drain(self):
        for phase in range(3):
            for copy in (self.through, self.straight, self.onward):
                copy(phase).wait_send()


class TapSum:
    def __init__(self, torus, color, slots, send, recv):
        self.torus, self.color, self.slots, self.send, self.recv = torus, color, slots, send, recv
        self.order = ORDERS[color]

    def copies(self, phase):
        axis = self.order[phase]
        here = self.slots.at[self.color, phase, self.torus.at[axis]]
        base = (self.color * 3 + phase) * 3
        return [
            pltpu.make_async_remote_copy(
                src_ref=here,
                dst_ref=here,
                send_sem=self.send.at[base + by - 1],
                recv_sem=self.recv.at[base + by - 1],
                device_id=self.torus.peer(axis, by),
                device_id_type=MESH,
            )
            for by in (1, 2, 3)
        ]

    def begin(self, phase, value):
        self.slots[self.color, phase, self.torus.at[self.order[phase]]] = value
        for copy in self.copies(phase):
            copy.start()

    def finish(self, phase):
        for copy in self.copies(phase):
            copy.wait_recv()
        slots = self.slots
        total = slots[self.color, phase, 0]
        for place in (1, 2, 3):
            total = total + slots[self.color, phase, place]
        return total

    def drain(self):
        for phase in range(3):
            for copy in self.copies(phase):
                copy.wait_send()


def reduce_kernel(grads, taps, out, taps_out, *scratch):
    landed = [scratch[3 * c : 3 * c + 3] for c in range(3)]
    sums = [scratch[9 + 2 * c : 11 + 2 * c] for c in range(3)]
    slots, send, recv, tap_send, tap_recv = scratch[15:]
    torus = Torus()
    greet(torus)
    tap_sums = [TapSum(torus, color, slots, tap_send, tap_recv) for color in range(3)]
    groups = [
        [Scatter(torus, grad, strip, grads, landed, sums, out, send, recv) for strip in range(6)]
        for grad in range(GRADS)
    ]
    for tap_sum in tap_sums:
        tap_sum.begin(0, taps[:, 256 * tap_sum.color : 256 * tap_sum.color + 256])
    for group in groups:
        for one in group:
            one.begin(0)
    for phase in range(3):
        for tap_sum in tap_sums:
            total = tap_sum.finish(phase)
            if phase < 2:
                tap_sum.begin(phase + 1, total)
            else:
                taps_out[:, 256 * tap_sum.color : 256 * tap_sum.color + 256] = total
        for group in groups:
            for one in group:
                one.relay(phase)
        for group in groups:
            for one in group:
                one.finish(phase)
                if phase < 2:
                    one.begin(phase + 1)
    for one in [one for group in groups for one in group] + tap_sums:
        one.drain()


def reduce_all(grads, taps):
    vmem = pl.BlockSpec(memory_space=pltpu.VMEM)
    landed = [
        pltpu.VMEM((GRADS, 2, 3) + dims + (24, 128), BF16) for order in ORDERS for dims in LEFT[order]
    ]
    sums = [
        pltpu.VMEM((GRADS, 2) + dims + (24, 128), BF16)
        for order in ORDERS
        for dims in LEFT[order][:2]
    ]
    copies = GRADS * 6 * 9
    return pl.pallas_call(
        reduce_kernel,
        out_shape=(
            jax.ShapeDtypeStruct((GRADS, 24, 768), F32),
            jax.ShapeDtypeStruct((32, 768), F32),
        ),
        in_specs=[vmem, vmem],
        out_specs=(vmem, vmem),
        scratch_shapes=landed
        + sums
        + [
            pltpu.VMEM((3, 3, 4, 32, 256), F32),
            pltpu.SemaphoreType.DMA((copies,)),
            pltpu.SemaphoreType.DMA((copies,)),
            pltpu.SemaphoreType.DMA((27,)),
            pltpu.SemaphoreType.DMA((27,)),
        ],
        compiler_params=pltpu.CompilerParams(
            collective_id=0, has_side_effects=True, vmem_limit_bytes=60 << 20
        ),
    )(grads, taps)


def strips(term):
    return term.astype(BF16).reshape(1536, 6, 128).transpose(1, 0, 2).reshape(6, 2, 4, 4, 2, 24, 128)


def padded_2(shard, sides, width):
    for axis, dim in sides:
        peers, length = (lax.axis_size(axis), shard.shape[dim])
        up = [(i, (i + 1) % peers) for i in range(peers - 1)]
        down = [(j, i) for i, j in up]
        last = lax.slice_in_dim(shard, length - width, length, axis=dim)
        leading = lax.slice_in_dim(shard, 0, width, axis=dim)
        before = lax.ppermute(last, axis, up)
        after = lax.ppermute(leading, axis, down)
        shard = jnp.concatenate([before, shard, after], axis=dim)
    return shard


def layer_normalizer(values):
    center = values - jnp.mean(values, axis=-1, keepdims=True)
    inverse = lax.rsqrt(jnp.mean(center * center, axis=-1, keepdims=True) + epsilon)
    return (center * inverse, inverse)


def shards(inputs, lengths, cotangent, w_value, w_gate, kernel, w_out):
    frame_total = inputs[0]
    count = frame_total.shape[0]
    channel_total = frame_total.shape[1]
    channel_width = channel_total * lax.axis_size("tensor")
    taps_count = kernel.shape[0]
    half = (taps_count - 1) // 2
    tensor_position = lax.axis_index("tensor")
    first_frame = lax.axis_index("seq") * count
    positions = first_frame + jnp.arange(count, dtype=jnp.int32)
    valid = (positions < lengths[0]).astype(jnp.float32)[:, None]
    taps = kernel.astype(jnp.float32)
    complete_rows = lax.all_gather(frame_total, "tensor", axis=1, tiled=True)
    centered_scaled, inverse_deviation_one = layer_normalizer(complete_rows.astype(jnp.float32))
    normalized_rows = centered_scaled.astype(jnp.bfloat16)
    values = jnp.dot(normalized_rows, w_value, preferred_element_type=jnp.float32)
    gates = jnp.dot(normalized_rows, w_gate, preferred_element_type=jnp.float32)
    sigma = jax.nn.sigmoid(gates)
    hidden = (values * sigma * valid).astype(jnp.bfloat16)
    padded = padded_2(hidden, (("seq", 0),), half).astype(jnp.float32)
    conv = jnp.zeros((count, channel_total), jnp.float32)
    for offset in range(taps_count):
        conv = conv + padded[offset : offset + count] * taps[offset]
    conv_sum, conv_square = lax.psum(
        (jnp.sum(conv, axis=-1), jnp.sum(conv * conv, axis=-1)), "tensor"
    )
    conv_mean = (conv_sum / channel_width)[:, None]
    conv_var = (conv_square / channel_width)[:, None] - conv_mean * conv_mean
    rstd_two = lax.rsqrt(conv_var + epsilon)
    zhat = (conv - conv_mean) * rstd_two
    swish_gate = jax.nn.sigmoid(zhat)
    swished = (zhat * swish_gate).astype(jnp.bfloat16)
    partial_out = jnp.dot(swished, w_out, preferred_element_type=jnp.float32)
    summed = lax.psum_scatter(
        partial_out.astype(jnp.bfloat16), "tensor", scatter_dimension=1, tiled=True
    ).astype(jnp.float32)
    output = (frame_total.astype(jnp.float32) + summed).astype(jnp.bfloat16)
    upstream = cotangent[0]
    upstream_whole = lax.all_gather(upstream, "tensor", axis=1, tiled=True)
    out_term = jnp.dot(upstream_whole.T, swished, preferred_element_type=jnp.float32)
    dswish = jnp.dot(upstream_whole, w_out.T, preferred_element_type=jnp.float32)
    dswish = dswish * (swish_gate + zhat * swish_gate * (1.0 - swish_gate))
    slope_sum, slope_cross = lax.psum(
        (jnp.sum(dswish, axis=-1), jnp.sum(dswish * zhat, axis=-1)), "tensor"
    )
    dconv = rstd_two * (
        dswish
        - (slope_sum / channel_width)[:, None]
        - zhat * (slope_cross / channel_width)[:, None]
    )
    dconv = dconv.astype(jnp.bfloat16)
    slope = dconv.astype(jnp.float32)
    kernel_term = jnp.stack(
        [jnp.sum(padded[offset : offset + count] * slope, axis=0) for offset in range(taps_count)]
    )
    slope_pad = padded_2(dconv, (("seq", 0),), half).astype(jnp.float32)
    dhidden = jnp.zeros((count, channel_total), jnp.float32)
    for offset in range(taps_count):
        dhidden = dhidden + slope_pad[2 * half - offset : 2 * half - offset + count] * taps[offset]
    dhidden = dhidden * valid
    dvalues = (dhidden * sigma).astype(jnp.bfloat16)
    dgates = (dhidden * values * sigma * (1.0 - sigma)).astype(jnp.bfloat16)
    value_term = jnp.dot(normalized_rows.T, dvalues, preferred_element_type=jnp.float32)
    gate_term = jnp.dot(normalized_rows.T, dgates, preferred_element_type=jnp.float32)
    dnormed_part = jnp.dot(dvalues, w_value.T, preferred_element_type=jnp.float32) + jnp.dot(
        dgates, w_gate.T, preferred_element_type=jnp.float32
    )
    normalized_grad = lax.psum_scatter(
        dnormed_part.astype(jnp.bfloat16), "tensor", scatter_dimension=1, tiled=True
    ).astype(jnp.float32)
    local_centered_scaled = lax.dynamic_slice_in_dim(
        centered_scaled, tensor_position * channel_total, channel_total, 1
    )
    input_total_sum, input_cross_term = lax.psum(
        (
            jnp.sum(normalized_grad, axis=-1),
            jnp.sum(normalized_grad * local_centered_scaled, axis=-1),
        ),
        "tensor",
    )
    input_gradient = upstream.astype(jnp.float32) + inverse_deviation_one * (
        normalized_grad
        - (input_total_sum / channel_width)[:, None]
        - local_centered_scaled * (input_cross_term / channel_width)[:, None]
    )
    input_gradient = input_gradient.astype(jnp.bfloat16)
    reduced, kernel_grad = reduce_all(
        jnp.stack([strips(value_term), strips(gate_term), strips(out_term)]),
        jnp.pad(kernel_term, ((0, 1), (0, 0))),
    )
    kernel_grad = kernel_grad[:taps_count]
    value_grad, gate_grad, out_grad = reduced[0], reduced[1], reduced[2].T
    return (output[None], input_gradient[None], value_grad, gate_grad, kernel_grad, out_grad)


def solution(mesh):
    return jax.shard_map(
        shards,
        mesh=mesh,
        in_specs=(
            P("dp", "seq", "tensor"),
            P("dp"),
            P("dp", "seq", "tensor"),
            P(None, "tensor"),
            P(None, "tensor"),
            P(None, "tensor"),
            P("tensor", None),
        ),
        out_specs=(
            P("dp", "seq", "tensor"),
            P("dp", "seq", "tensor"),
            P(("seq", "dp"), "tensor"),
            P(("seq", "dp"), "tensor"),
            P(None, "tensor"),
            P("tensor", ("seq", "dp")),
        ),
        check_vma=False,
    )
```

```python
import functools

import jax
import jax.numpy as jnp
from jax import lax
from jax.experimental import pallas as pl
from jax.experimental.pallas import tpu as pltpu
from jax.sharding import PartitionSpec as P

epsilon = 1e-05
MESH = pl.DeviceIdType.MESH
BF16, F32 = jnp.bfloat16, jnp.float32
ORDERS = ("xyz", "yzx", "zxy")
GRADS = 3
FRAMES, WIDTH, HALF = 768, 1536, 768
ROWS, CHUNKS = 256, 3
GROUP = 16
SPREAD = ROWS // 8
TAPS, REACH, EDGE = 31, 15, 16
LEFT = {
    "xyz": ((4, 4), (4,), ()),
    "yzx": ((2, 4, 2), (2, 2), ()),
    "zxy": ((2, 4, 2), (4,), ()),
}


class Torus:
    def __init__(self):
        seq, low = lax.axis_index("seq"), lax.axis_index("dp")
        self.at = {
            "x": lax.div(seq, 16) * 2 + low,
            "y": lax.rem(seq, 4),
            "z": lax.rem(lax.div(seq, 4), 4),
        }

    def moved(self, axis, by):
        return lax.rem(self.at[axis] + (by + 4), 4)

    def beside(self, by):
        return {"seq": lax.rem(lax.axis_index("seq") + (by + 32), 32)}

    def peer(self, axis, by):
        at = dict(self.at)
        at[axis] = self.moved(axis, by)
        return {
            "seq": (lax.div(at["x"], 2) * 4 + at["z"]) * 4 + at["y"],
            "dp": lax.rem(at["x"], 2),
        }


def part_of(order, phase, coord):
    every = slice(None)
    high, low = lax.div(coord, 2), lax.rem(coord, 2)
    if phase == 0:
        return {
            "x": (high, every, every, low),
            "y": (every, every, coord, every),
            "z": (every, coord, every, every),
        }[order[0]]
    if phase == 1:
        return {"xyz": (every, coord), "yzx": (every, coord, every), "zxy": (high, every, low)}[order]
    return {"xyz": (coord,), "yzx": (high, low), "zxy": (coord,)}[order]


class Scatter:
    def __init__(self, torus, grad, strip, source, landed, sums, out, send, recv):
        self.torus, self.grad, self.strip = torus, grad, strip
        self.source, self.landed, self.sums, self.out = source, landed, sums, out
        self.send, self.recv = send, recv
        self.order = ORDERS[strip // 2]
        self.way = 1 if strip % 2 == 0 else -1

    def held(self, phase, coord):
        part = part_of(self.order, phase, coord)
        if phase == 0:
            return self.source.at[(self.grad, self.strip) + part]
        return self.sums[self.strip // 2][phase - 1].at[(self.grad, self.strip % 2) + part]

    def slot(self, phase, which):
        return self.landed[self.strip // 2][phase].at[self.grad, self.strip % 2, which]

    def copy(self, phase, which, ref, by):
        number = ((self.grad * 6 + self.strip) * 3 + phase) * 3 + which
        return pltpu.make_async_remote_copy(
            src_ref=ref,
            dst_ref=self.slot(phase, which),
            send_sem=self.send.at[number],
            recv_sem=self.recv.at[number],
            device_id=self.torus.peer(self.order[phase], by),
            device_id_type=MESH,
        )

    def place(self, phase, by):
        return self.torus.moved(self.order[phase], by)

    def through(self, phase):
        return self.copy(phase, 0, self.held(phase, self.place(phase, 2)), self.way)

    def straight(self, phase):
        return self.copy(phase, 1, self.held(phase, self.place(phase, -self.way)), -self.way)

    def onward(self, phase):
        return self.copy(phase, 2, self.slot(phase, 0), self.way)

    def begin(self, phase):
        self.through(phase).start()
        self.straight(phase).start()

    def relay(self, phase):
        self.through(phase).wait_recv()
        slot = self.slot(phase, 0)
        mine = self.held(phase, self.place(phase, self.way))
        slot[...] = (slot[...].astype(F32) + mine[...].astype(F32)).astype(BF16)
        self.onward(phase).start()

    def finish(self, phase):
        self.straight(phase).wait_recv()
        self.onward(phase).wait_recv()
        mine = self.held(phase, self.torus.at[self.order[phase]])
        total = (
            mine[...].astype(F32)
            + self.slot(phase, 1)[...].astype(F32)
            + self.slot(phase, 2)[...].astype(F32)
        )
        if phase < 2:
            self.sums[self.strip // 2][phase][self.grad, self.strip % 2] = total.astype(BF16)
        else:
            self.out[self.grad][:, 128 * self.strip : 128 * self.strip + 128] = total

    def drain(self):
        for phase in range(3):
            for copy in (self.through, self.straight, self.onward):
                copy(phase).wait_send()


class TapSum:
    def __init__(self, torus, color, slots, send, recv):
        self.torus, self.color, self.slots, self.send, self.recv = torus, color, slots, send, recv
        self.order = ORDERS[color]

    def copies(self, phase):
        axis = self.order[phase]
        here = self.slots.at[self.color, phase, self.torus.at[axis]]
        base = (self.color * 3 + phase) * 3
        return [
            pltpu.make_async_remote_copy(
                src_ref=here,
                dst_ref=here,
                send_sem=self.send.at[base + by - 1],
                recv_sem=self.recv.at[base + by - 1],
                device_id=self.torus.peer(axis, by),
                device_id_type=MESH,
            )
            for by in (1, 2, 3)
        ]

    def begin(self, phase, value):
        self.slots[self.color, phase, self.torus.at[self.order[phase]]] = value
        for copy in self.copies(phase):
            copy.start()

    def finish(self, phase):
        for copy in self.copies(phase):
            copy.wait_recv()
        slots = self.slots
        total = slots[self.color, phase, 0]
        for place in (1, 2, 3):
            total = total + slots[self.color, phase, place]
        return total

    def drain(self):
        for phase in range(3):
            for copy in self.copies(phase):
                copy.wait_send()


def greet(torus):
    barrier = pltpu.get_barrier_semaphore()
    peers = [torus.peer(axis, by) for axis in "xyz" for by in (1, 2, 3)]
    peers += [torus.beside(1), torus.beside(-1), {"tensor": 1 - lax.axis_index("tensor")}]
    for peer in peers:
        pl.semaphore_signal(barrier, inc=1, device_id=peer, device_id_type=MESH)
    pl.semaphore_wait(barrier, len(peers))


def sigmoid(values):
    return 0.5 * jnp.tanh(0.5 * values) + 0.5


def dot(a, b, contract):
    return lax.dot_general(a, b, (contract, ((), ())), preferred_element_type=F32)


def kernel(lengths, x, cot, w_value, w_gate, taps, w_out, out, grad_in, value_grad, gate_grad, taps_grad, out_grad, *scratch):
    landed = [scratch[3 * c : 3 * c + 3] for c in range(3)]
    sums = [scratch[9 + 2 * c : 11 + 2 * c] for c in range(3)]
    (
        slots, send, recv, tap_send, tap_recv,
        grads, xf, uf, wv, wg, wo, nb, rstd1, vb, sg, hb, db, cb, sw, ds, rstd2, stat_out, stat_in,
        dv, dg, po, part_out, part_in, tap_wide, tap_acc,
        load_sem, x_send, x_recv, u_send, u_recv, halo_send, halo_recv, stat_send, stat_recv, part_send, part_recv, store_sem,
    ) = scratch[15:]
    torus = Torus()
    me = lax.axis_index("tensor")
    other = 1 - me
    partner = {"tensor": other}
    seq = lax.axis_index("seq")

    def remote(src, dst, send_sem, recv_sem, to):
        return pltpu.make_async_remote_copy(
            src_ref=src, dst_ref=dst, send_sem=send_sem, recv_sem=recv_sem, device_id=to, device_id_type=MESH
        )

    def chunk(c):
        return pl.ds(ROWS * c, ROWS)

    def x_load(c):
        return pltpu.make_async_copy(x.at[chunk(c)], xf.at[me, chunk(c)], load_sem.at[c])

    def x_share(c):
        return remote(x.at[chunk(c)], xf.at[me, chunk(c)], x_send.at[c], x_recv.at[c], partner)

    u_load = pltpu.make_async_copy(cot, uf.at[me], load_sem.at[3])
    u_share = remote(cot, uf.at[me], u_send, u_recv, partner)
    wv_load = pltpu.make_async_copy(w_value, wv, load_sem.at[4])
    wg_load = pltpu.make_async_copy(w_gate, wg, load_sem.at[5])
    wo_loads = [
        pltpu.make_async_copy(w_out.at[:, pl.ds(HALF * h, HALF)], wo.at[h], load_sem.at[6 + h])
        for h in range(2)
    ]
    for c in range(CHUNKS):
        x_load(c).start()
    wv_load.start()
    wg_load.start()
    u_load.start()
    for load in wo_loads:
        load.start()
    greet(torus)
    for c in range(CHUNKS):
        x_share(c).start()
    u_share.start()

    tap_rows = taps[...].astype(F32)
    for j in range(6):
        for k in range(TAPS):
            tap_wide[j, k] = jnp.broadcast_to(tap_rows[k : k + 1, 128 * j : 128 * j + 128], (8, 128))

    for c in range(CHUNKS):
        x_load(c).wait()
        x_share(c).wait_recv()

        def normalize(i, _, c=c):
            rows = pl.ds(pl.multiple_of(ROWS * c + GROUP * i, GROUP), GROUP)
            a, b = xf[0, rows, :].astype(F32), xf[1, rows, :].astype(F32)
            mean = (jnp.sum(a, -1, keepdims=True) + jnp.sum(b, -1, keepdims=True)) / WIDTH
            a, b = a - mean, b - mean
            var = (jnp.sum(a * a, -1, keepdims=True) + jnp.sum(b * b, -1, keepdims=True)) / WIDTH
            scale = lax.rsqrt(var + epsilon)
            nb[rows, 0:HALF] = (a * scale).astype(BF16)
            nb[rows, HALF:WIDTH] = (b * scale).astype(BF16)
            rstd1[rows, :] = jnp.broadcast_to(scale, (GROUP, 128))
            return 0

        lax.fori_loop(0, ROWS // GROUP, normalize, 0, unroll=2)

    wv_load.wait()
    wg_load.wait()
    length = lengths[0]

    def valid_rows(first, count):
        position = lax.broadcasted_iota(jnp.int32, (count, 128), 0) + (seq * FRAMES + first)
        return jnp.where(position < length, 1.0, 0.0)

    def gate(c):
        for n in range(3):
            columns = slice(256 * n, 256 * n + 256)
            values = jnp.dot(nb[chunk(c), :], wv[:, columns], preferred_element_type=F32)
            sigma = sigmoid(jnp.dot(nb[chunk(c), :], wg[:, columns], preferred_element_type=F32))
            valid = valid_rows(ROWS * c, ROWS)
            vb[chunk(c), columns] = values
            sg[chunk(c), columns] = sigma
            for half in range(2):
                strip = slice(128 * half, 128 * half + 128)
                hidden = values[:, strip] * sigma[:, strip] * valid
                hb[2 * n + half, pl.ds(EDGE + ROWS * c, ROWS), :] = hidden.astype(BF16).astype(F32)

    def halo(buf, number):
        first, last = pl.ds(EDGE, EDGE), pl.ds(FRAMES, EDGE)
        before, after = pl.ds(0, EDGE), pl.ds(FRAMES + EDGE, EDGE)
        return (
            remote(buf.at[:, first], buf.at[:, after], halo_send.at[number], halo_recv.at[number], torus.beside(-1)),
            remote(buf.at[:, last], buf.at[:, before], halo_send.at[number + 1], halo_recv.at[number + 1], torus.beside(1)),
        )

    def halo_end(copies, buf):
        inside = (
            jnp.where(seq < 31, 1.0, 0.0).astype(F32),
            jnp.where(seq > 0, 1.0, 0.0).astype(F32),
        )
        for copy, keep, rows in zip(copies, inside, (pl.ds(FRAMES + EDGE, EDGE), pl.ds(0, EDGE))):
            copy.wait_recv()
            buf[:, rows, :] = buf[:, rows, :] * keep

    gate(0)
    gate(2)
    h_halo = halo(hb, 0)
    for copy in h_halo:
        copy.start()
    gate(1)

    u_load.wait()
    u_share.wait_recv()
    for load in wo_loads:
        load.wait()
    for c in range(CHUNKS):
        for n in range(3):
            ds[chunk(c), 256 * n : 256 * n + 256] = dot(
                uf[0, chunk(c), :], wo[0, 256 * n : 256 * n + 256, :], ((1,), (1,))
            ) + dot(uf[1, chunk(c), :], wo[1, 256 * n : 256 * n + 256, :], ((1,), (1,)))

    def spread(buf, j, c, r):
        return buf[j, pl.ds(EDGE + ROWS * c + r, 8, stride=SPREAD), :]

    def convolve(buf, c, tap_at):
        def strip(j, _):
            for block in range(SPREAD // 8):
                totals = [None] * 8
                for m in range(8 + TAPS - 1):
                    shifted = spread(buf, j, c, 8 * block + m - REACH)
                    for i in range(max(0, m - TAPS + 1), min(8, m + 1)):
                        term = shifted * tap_wide[j, tap_at(m - i)]
                        totals[i] = term if totals[i] is None else totals[i] + term
                for i in range(8):
                    cb[j, pl.ds(ROWS * c + 8 * block + i, 8, stride=SPREAD), :] = totals[i]
            return 0

        lax.fori_loop(0, 6, strip, 0)

    lane = lax.broadcasted_iota(jnp.int32, (GROUP, 128), 1)

    def stat_copy(number, c):
        at = 3 * number + c
        return remote(
            stat_out.at[number, chunk(c)], stat_in.at[number, chunk(c)], stat_send.at[at], stat_recv.at[at], partner
        )

    def put_stats(number, rows, first, second):
        stat_out[number, rows, :] = jnp.where(lane < 64, first, second)

    def get_stats(number, rows):
        total = (stat_out[number, rows, :] + stat_in[number, rows, :]) * (1.0 / WIDTH)
        return total[:, 0:1], total[:, 64:65]

    def groups(c, body, unroll=2):
        def one(i, _):
            body(pl.multiple_of(ROWS * c + GROUP * i, GROUP))
            return 0

        lax.fori_loop(0, ROWS // GROUP, one, 0, unroll=unroll)

    def conv_stats(c):
        def body(first):
            rows = pl.ds(first, GROUP)
            strips = [cb[j, rows, :] for j in range(6)]
            total, square = strips[0], strips[0] * strips[0]
            for strip in strips[1:]:
                total, square = total + strip, square + strip * strip
            put_stats(0, rows, jnp.sum(total, -1, keepdims=True), jnp.sum(square, -1, keepdims=True))

        groups(c, body)
        stat_copy(0, c).start()

    for c in (1, 0, 2):
        if c == 0:
            halo_end(h_halo, hb)
        convolve(hb, c, lambda k: k)
        conv_stats(c)

    def activate(c):
        stat_copy(0, c).wait_recv()

        def body(first):
            rows = pl.ds(first, GROUP)
            mean, square = get_stats(0, rows)
            scale = lax.rsqrt(square - mean * mean + epsilon)
            rstd2[rows, :] = jnp.broadcast_to(scale, (GROUP, 128))
            total = cross = None
            for j in range(6):
                columns = slice(128 * j, 128 * j + 128)
                zhat = (cb[j, rows, :] - mean) * scale
                s = sigmoid(zhat)
                cb[j, rows, :] = zhat
                swish = zhat * s
                sw[rows, columns] = swish.astype(BF16)
                slope = ds[rows, columns] * (s + swish * (1.0 - s))
                ds[rows, columns] = slope
                total = slope if total is None else total + slope
                cross = slope * zhat if cross is None else cross + slope * zhat
            put_stats(1, rows, jnp.sum(total, -1, keepdims=True), jnp.sum(cross, -1, keepdims=True))

        groups(c, body)
        stat_copy(1, c).start()

    for c in (1, 0, 2):
        activate(c)

    def part_copy(number, c):
        at = 3 * number + c
        return remote(
            part_out.at[number, chunk(c)], part_in.at[number, chunk(c)], part_send.at[at], part_recv.at[at], partner
        )

    for c in range(CHUNKS):
        for n in range(3):
            part_out[0, chunk(c), 256 * n : 256 * n + 256] = jnp.dot(
                sw[chunk(c), :], wo[other, :, 256 * n : 256 * n + 256], preferred_element_type=F32
            ).astype(BF16)
        part_copy(0, c).start()
    for c in range(CHUNKS):
        for n in range(3):
            po[chunk(c), 256 * n : 256 * n + 256] = jnp.dot(
                sw[chunk(c), :], wo[me, :, 256 * n : 256 * n + 256], preferred_element_type=F32
            )

    finals = (value_grad, gate_grad, out_grad)
    scatters = [
        [Scatter(torus, g, j, grads, landed, sums, finals, send, recv) for j in range(6)] for g in range(GRADS)
    ]

    def weight_grad(g, rows_of, right, n):
        for m in range(4):
            term = dot(rows_of(m), right[:, 256 * n : 256 * n + 256], ((0,), (0,)))
            for half in range(2):
                grads[g, 2 * n + half, m // 2, 2 * (m % 2) : 2 * (m % 2) + 2] = (
                    term[:, 128 * half : 128 * half + 128].reshape(2, 4, 2, 24, 128).astype(BF16)
                )
        for half in range(2):
            scatters[g][2 * n + half].begin(0)

    for n in range(3):
        weight_grad(2, lambda m: uf[m // 2, :, 384 * (m % 2) : 384 * (m % 2) + 384], sw, n)

    def conv_slope(c):
        stat_copy(1, c).wait_recv()

        def body(first):
            rows = pl.ds(first, GROUP)
            mean, cross = get_stats(1, rows)
            scale = rstd2[rows, :]
            for j in range(6):
                slope = scale * (ds[rows, 128 * j : 128 * j + 128] - mean - cb[j, rows, :] * cross)
                db[j, pl.ds(pl.multiple_of(first + EDGE, GROUP), GROUP), :] = slope.astype(BF16).astype(F32)

        groups(c, body)

    conv_slope(0)
    conv_slope(2)
    d_halo = halo(db, 2)
    for copy in d_halo:
        copy.start()
    conv_slope(1)

    def tap_terms(j, _):
        totals = [jnp.zeros((8, 128), F32) for _ in range(TAPS)]
        for c in range(CHUNKS):
            for block in range(SPREAD // 8):
                slopes = [spread(db, j, c, 8 * block + i) for i in range(8)]
                for m in range(8 + TAPS - 1):
                    shifted = spread(hb, j, c, 8 * block + m - REACH)
                    for i in range(max(0, m - TAPS + 1), min(8, m + 1)):
                        totals[m - i] = totals[m - i] + shifted * slopes[i]
        for k in range(TAPS):
            tap_acc[j, k, :] = jnp.sum(totals[k], 0)
        tap_acc[j, TAPS, :] = jnp.zeros((128,), F32)
        return 0

    lax.fori_loop(0, 6, tap_terms, 0)
    tap_sums = [TapSum(torus, color, slots, tap_send, tap_recv) for color in range(3)]
    for color in range(3):
        tap_sums[color].begin(0, tap_acc[2 * color : 2 * color + 2])

    def relay(g, phase):
        for one in scatters[g]:
            one.relay(phase)

    def finish(g, phase):
        for one in scatters[g]:
            one.finish(phase)
            if phase < 2:
                one.begin(phase + 1)

    def tap_step(phase):
        for color in range(3):
            total = tap_sums[color].finish(phase)
            if phase < 2:
                tap_sums[color].begin(phase + 1, total)
            else:
                for half in range(2):
                    j = 2 * color + half
                    taps_grad[:, 128 * j : 128 * j + 128] = total[half]

    relay(2, 0)

    def gate_slopes(c):
        def body(first):
            rows = pl.ds(first, GROUP)
            valid = valid_rows(first, GROUP)
            for j in range(6):
                columns = slice(128 * j, 128 * j + 128)
                sigma = sg[rows, columns]
                slope = cb[j, rows, :] * valid * sigma
                dv[rows, columns] = slope.astype(BF16)
                dg[rows, columns] = (slope * vb[rows, columns] * (1.0 - sigma)).astype(BF16)

        groups(c, body)

    for c in (1, 0, 2):
        if c == 0:
            halo_end(d_halo, db)
        convolve(db, c, lambda k: TAPS - 1 - k)
        gate_slopes(c)
        if c == 1:
            finish(2, 0)
            tap_step(0)
        elif c == 0:
            relay(2, 1)
            tap_step(1)
        else:
            finish(2, 1)
            tap_step(2)

    for n in range(3):
        weight_grad(0, lambda m: nb[:, 384 * m : 384 * m + 384], dv, n)
    relay(2, 2)
    for n in range(3):
        weight_grad(1, lambda m: nb[:, 384 * m : 384 * m + 384], dg, n)
    finish(2, 2)

    def features(c, n, half):
        rows = pl.ds(pl.multiple_of(half * HALF + 256 * n, 256), 256)
        return dot(dv[chunk(c), :], wv[rows, :], ((1,), (1,))) + dot(dg[chunk(c), :], wg[rows, :], ((1,), (1,)))

    for c in range(CHUNKS):
        for n in range(3):
            part_out[1, chunk(c), 256 * n : 256 * n + 256] = features(c, n, other).astype(BF16)
        part_copy(1, c).start()
    relay(0, 0)
    for c in range(CHUNKS):
        for n in range(3):
            vb[chunk(c), 256 * n : 256 * n + 256] = features(c, n, me)
    relay(1, 0)

    def output_rows(c):
        part_copy(0, c).wait_recv()

        def body(first):
            rows = pl.ds(first, GROUP)
            total = xf[me, rows, :].astype(F32) + (po[rows, :] + part_in[0, rows, :].astype(F32))
            xf[me, rows, :] = total.astype(BF16)

        groups(c, body)
        store = pltpu.make_async_copy(xf.at[me, chunk(c)], out.at[chunk(c)], store_sem.at[c])
        store.start()
        return store

    def feature_stats(c):
        part_copy(1, c).wait_recv()

        def body(first):
            rows = pl.ds(first, GROUP)
            slope = vb[rows, :] + part_in[1, rows, :].astype(F32)
            vb[rows, :] = slope
            unit = nb[rows, pl.ds(pl.multiple_of(me * HALF, HALF), HALF)].astype(F32)
            put_stats(2, rows, jnp.sum(slope, -1, keepdims=True), jnp.sum(slope * unit, -1, keepdims=True))

        groups(c, body)
        stat_copy(2, c).start()

    def input_rows(c):
        stat_copy(2, c).wait_recv()

        def body(first):
            rows = pl.ds(first, GROUP)
            mean, cross = get_stats(2, rows)
            scale = rstd1[rows, 0:1]
            unit = nb[rows, pl.ds(pl.multiple_of(me * HALF, HALF), HALF)].astype(F32)
            total = uf[me, rows, :].astype(F32) + scale * (vb[rows, :] - mean - unit * cross)
            uf[me, rows, :] = total.astype(BF16)

        groups(c, body)
        store = pltpu.make_async_copy(uf.at[me, chunk(c)], grad_in.at[chunk(c)], store_sem.at[3 + c])
        store.start()
        return store

    for c in range(CHUNKS):
        feature_stats(c)
    stores = [output_rows(c) for c in range(CHUNKS)]
    finish(0, 0)
    stores += [input_rows(c) for c in range(CHUNKS)]
    finish(1, 0)
    for phase in (1, 2):
        for g in (0, 1):
            relay(g, phase)
        for g in (0, 1):
            finish(g, phase)

    for group in scatters:
        for one in group:
            one.drain()
    for one in tap_sums:
        one.drain()
    for store in stores:
        store.wait()
    for copy in [x_share(c) for c in range(CHUNKS)] + [u_share]:
        copy.wait_send()
    for copy in h_halo + d_halo:
        copy.wait_send()
    for number in range(3):
        for c in range(CHUNKS):
            stat_copy(number, c).wait_send()
    for number in range(2):
        for c in range(CHUNKS):
            part_copy(number, c).wait_send()


def scratch_shapes():
    vmem, dma = pltpu.VMEM, pltpu.SemaphoreType.DMA
    shapes = [vmem((GRADS, 2, 3) + dims + (24, 128), BF16) for order in ORDERS for dims in LEFT[order]]
    shapes += [vmem((GRADS, 2) + dims + (24, 128), BF16) for order in ORDERS for dims in LEFT[order][:2]]
    copies = GRADS * 6 * 9
    shapes += [vmem((3, 3, 4, 2, 32, 128), F32), dma((copies,)), dma((copies,)), dma((27,)), dma((27,))]
    square, padded = (FRAMES, HALF), (6, FRAMES + 2 * EDGE, 128)
    shapes += [
        vmem((GRADS, 6, 2, 4, 4, 2, 24, 128), BF16),
        vmem((2,) + square, BF16),
        vmem((2,) + square, BF16),
        vmem((WIDTH, HALF), BF16),
        vmem((WIDTH, HALF), BF16),
        vmem((2,) + square, BF16),
        vmem((FRAMES, WIDTH), BF16),
        vmem((FRAMES, 128), F32),
        vmem(square, F32),
        vmem(square, F32),
        vmem(padded, F32),
        vmem(padded, F32),
        vmem((6, FRAMES, 128), F32),
        vmem(square, BF16),
        vmem(square, F32),
        vmem((FRAMES, 128), F32),
        vmem((3, FRAMES, 128), F32),
        vmem((3, FRAMES, 128), F32),
        vmem(square, BF16),
        vmem(square, BF16),
        vmem(square, F32),
        vmem((2,) + square, BF16),
        vmem((2,) + square, BF16),
        vmem((6, TAPS, 8, 128), F32),
        vmem((6, TAPS + 1, 128), F32),
        dma((8,)), dma((3,)), dma((3,)), dma(()), dma(()), dma((4,)), dma((4,)),
        dma((9,)), dma((9,)), dma((6,)), dma((6,)), dma((6,)),
    ]
    return shapes


def shards(inputs, lengths, cotangent, w_value, w_gate, kernel_taps, w_out):
    here, vmem = pl.BlockSpec(memory_space=pl.ANY), pl.BlockSpec(memory_space=pltpu.VMEM)
    smem = pl.BlockSpec(memory_space=pltpu.SMEM)
    rows = jax.ShapeDtypeStruct((FRAMES, HALF), BF16)
    block = jax.ShapeDtypeStruct((24, HALF), F32)
    output, input_gradient, value_grad, gate_grad, kernel_grad, out_grad = pl.pallas_call(
        kernel,
        out_shape=(rows, rows, block, block, jax.ShapeDtypeStruct((TAPS + 1, HALF), F32), block),
        in_specs=[smem, here, here, here, here, vmem, here],
        out_specs=(here, here, vmem, vmem, vmem, vmem),
        scratch_shapes=scratch_shapes(),
        compiler_params=pltpu.CompilerParams(
            collective_id=0, has_side_effects=True, vmem_limit_bytes=67043328
        ),
    )(lengths, inputs[0], cotangent[0], w_value, w_gate, kernel_taps, w_out)
    return (output[None], input_gradient[None], value_grad, gate_grad, kernel_grad[:TAPS], out_grad.T)


def solution(mesh):
    return jax.shard_map(
        shards,
        mesh=mesh,
        in_specs=(
            P("dp", "seq", "tensor"),
            P("dp"),
            P("dp", "seq", "tensor"),
            P(None, "tensor"),
            P(None, "tensor"),
            P(None, "tensor"),
            P("tensor", None),
        ),
        out_specs=(
            P("dp", "seq", "tensor"),
            P("dp", "seq", "tensor"),
            P(("seq", "dp"), "tensor"),
            P(("seq", "dp"), "tensor"),
            P(None, "tensor"),
            P("tensor", ("seq", "dp")),
        ),
        check_vma=False,
    )
```

```python
import functools

import jax
import jax.numpy as jnp
from jax import lax
from jax.experimental import pallas as pl
from jax.experimental.pallas import tpu as pltpu
from jax.sharding import PartitionSpec as P

epsilon = 1e-05
MESH = pl.DeviceIdType.MESH
BF16, F32 = jnp.bfloat16, jnp.float32
ORDERS = ("xyz", "yzx", "zxy")
GRADS = 3
FRAMES, WIDTH, HALF = 768, 1536, 768
ROWS, CHUNKS = 256, 3
GROUP = 16
BLOCK = 32
TAPS, REACH, EDGE = 31, 15, 16
LEFT = {
    "xyz": ((4, 4), (4,), ()),
    "yzx": ((2, 4, 2), (2, 2), ()),
    "zxy": ((2, 4, 2), (4,), ()),
}


class Torus:
    def __init__(self):
        seq, low = lax.axis_index("seq"), lax.axis_index("dp")
        self.at = {
            "x": lax.div(seq, 16) * 2 + low,
            "y": lax.rem(seq, 4),
            "z": lax.rem(lax.div(seq, 4), 4),
        }

    def moved(self, axis, by):
        return lax.rem(self.at[axis] + (by + 4), 4)

    def beside(self, by):
        return {"seq": lax.rem(lax.axis_index("seq") + (by + 32), 32)}

    def peer(self, axis, by):
        at = dict(self.at)
        at[axis] = self.moved(axis, by)
        return {
            "seq": (lax.div(at["x"], 2) * 4 + at["z"]) * 4 + at["y"],
            "dp": lax.rem(at["x"], 2),
        }


def part_of(order, phase, coord):
    every = slice(None)
    high, low = lax.div(coord, 2), lax.rem(coord, 2)
    if phase == 0:
        return {
            "x": (high, every, every, low),
            "y": (every, every, coord, every),
            "z": (every, coord, every, every),
        }[order[0]]
    if phase == 1:
        return {"xyz": (every, coord), "yzx": (every, coord, every), "zxy": (high, every, low)}[order]
    return {"xyz": (coord,), "yzx": (high, low), "zxy": (coord,)}[order]


class Scatter:
    def __init__(self, torus, grad, strip, source, landed, sums, out, send, recv):
        self.torus, self.grad, self.strip = torus, grad, strip
        self.source, self.landed, self.sums, self.out = source, landed, sums, out
        self.send, self.recv = send, recv
        self.order = ORDERS[strip // 2]
        self.way = 1 if strip % 2 == 0 else -1

    def held(self, phase, coord):
        part = part_of(self.order, phase, coord)
        if phase == 0:
            return self.source.at[(self.grad, self.strip) + part]
        return self.sums[self.strip // 2][phase - 1].at[(self.grad, self.strip % 2) + part]

    def slot(self, phase, which):
        return self.landed[self.strip // 2][phase].at[self.grad, self.strip % 2, which]

    def copy(self, phase, which, ref, by):
        number = ((self.grad * 6 + self.strip) * 3 + phase) * 3 + which
        return pltpu.make_async_remote_copy(
            src_ref=ref,
            dst_ref=self.slot(phase, which),
            send_sem=self.send.at[number],
            recv_sem=self.recv.at[number],
            device_id=self.torus.peer(self.order[phase], by),
            device_id_type=MESH,
        )

    def place(self, phase, by):
        return self.torus.moved(self.order[phase], by)

    def through(self, phase):
        return self.copy(phase, 0, self.held(phase, self.place(phase, 2)), self.way)

    def straight(self, phase):
        return self.copy(phase, 1, self.held(phase, self.place(phase, -self.way)), -self.way)

    def onward(self, phase):
        return self.copy(phase, 2, self.slot(phase, 0), self.way)

    def begin(self, phase):
        self.through(phase).start()
        self.straight(phase).start()

    def relay(self, phase):
        self.through(phase).wait_recv()
        slot = self.slot(phase, 0)
        mine = self.held(phase, self.place(phase, self.way))
        slot[...] = (slot[...].astype(F32) + mine[...].astype(F32)).astype(BF16)
        self.onward(phase).start()

    def finish(self, phase):
        self.straight(phase).wait_recv()
        self.onward(phase).wait_recv()
        mine = self.held(phase, self.torus.at[self.order[phase]])
        total = (
            mine[...].astype(F32)
            + self.slot(phase, 1)[...].astype(F32)
            + self.slot(phase, 2)[...].astype(F32)
        )
        if phase < 2:
            self.sums[self.strip // 2][phase][self.grad, self.strip % 2] = total.astype(BF16)
        else:
            self.out[self.grad][:, 128 * self.strip : 128 * self.strip + 128] = total

    def drain(self):
        for phase in range(3):
            for copy in (self.through, self.straight, self.onward):
                copy(phase).wait_send()


class TapSum:
    def __init__(self, torus, color, slots, send, recv):
        self.torus, self.color, self.slots, self.send, self.recv = torus, color, slots, send, recv
        self.order = ORDERS[color]

    def copies(self, phase):
        axis = self.order[phase]
        here = self.slots.at[self.color, phase, self.torus.at[axis]]
        base = (self.color * 3 + phase) * 3
        return [
            pltpu.make_async_remote_copy(
                src_ref=here,
                dst_ref=here,
                send_sem=self.send.at[base + by - 1],
                recv_sem=self.recv.at[base + by - 1],
                device_id=self.torus.peer(axis, by),
                device_id_type=MESH,
            )
            for by in (1, 2, 3)
        ]

    def begin(self, phase, value):
        self.slots[self.color, phase, self.torus.at[self.order[phase]]] = value
        for copy in self.copies(phase):
            copy.start()

    def finish(self, phase):
        for copy in self.copies(phase):
            copy.wait_recv()
        slots = self.slots
        total = slots[self.color, phase, 0]
        for place in (1, 2, 3):
            total = total + slots[self.color, phase, place]
        return total

    def drain(self):
        for phase in range(3):
            for copy in self.copies(phase):
                copy.wait_send()


def greet(torus):
    barrier = pltpu.get_barrier_semaphore()
    peers = [torus.peer(axis, by) for axis in "xyz" for by in (1, 2, 3)]
    peers += [torus.beside(1), torus.beside(-1), {"tensor": 1 - lax.axis_index("tensor")}]
    for peer in peers:
        pl.semaphore_signal(barrier, inc=1, device_id=peer, device_id_type=MESH)
    pl.semaphore_wait(barrier, len(peers))


def sigmoid(values):
    return 0.5 * jnp.tanh(0.5 * values) + 0.5


def dot(a, b, contract):
    return lax.dot_general(a, b, (contract, ((), ())), preferred_element_type=F32)


def kernel(lengths, x, cot, w_value, w_gate, taps, w_out, out, grad_in, value_grad, gate_grad, taps_grad, out_grad, *scratch):
    landed = [scratch[3 * c : 3 * c + 3] for c in range(3)]
    sums = [scratch[9 + 2 * c : 11 + 2 * c] for c in range(3)]
    (
        slots, send, recv, tap_send, tap_recv,
        grads, xf, uf, wv, wg, wo, nb, rstd1, vb, sg, hb, db, cb, sw, ds, rstd2, stat_out, stat_in,
        dv, dg, po, part_out, part_in, tap_wide, tap_acc,
        load_sem, x_send, x_recv, u_send, u_recv, halo_send, halo_recv, stat_send, stat_recv, part_send, part_recv, store_sem,
    ) = scratch[15:]
    torus = Torus()
    me = lax.axis_index("tensor")
    other = 1 - me
    partner = {"tensor": other}
    seq = lax.axis_index("seq")

    def remote(src, dst, send_sem, recv_sem, to):
        return pltpu.make_async_remote_copy(
            src_ref=src, dst_ref=dst, send_sem=send_sem, recv_sem=recv_sem, device_id=to, device_id_type=MESH
        )

    def chunk(c):
        return pl.ds(ROWS * c, ROWS)

    def x_load(c):
        return pltpu.make_async_copy(x.at[chunk(c)], xf.at[me, chunk(c)], load_sem.at[c])

    def x_share(c):
        return remote(x.at[chunk(c)], xf.at[me, chunk(c)], x_send.at[c], x_recv.at[c], partner)

    u_load = pltpu.make_async_copy(cot, uf.at[me], load_sem.at[3])
    u_share = remote(cot, uf.at[me], u_send, u_recv, partner)
    wv_load = pltpu.make_async_copy(w_value, wv, load_sem.at[4])
    wg_load = pltpu.make_async_copy(w_gate, wg, load_sem.at[5])
    wo_loads = [
        pltpu.make_async_copy(w_out.at[:, pl.ds(HALF * h, HALF)], wo.at[h], load_sem.at[6 + h])
        for h in range(2)
    ]
    for c in (0, 2, 1):
        x_load(c).start()
    wv_load.start()
    wg_load.start()
    u_load.start()
    for load in wo_loads:
        load.start()
    greet(torus)
    for c in (0, 2, 1):
        x_share(c).start()
    u_share.start()

    tap_rows = taps[...].astype(F32)
    for j in range(6):
        for k in range(TAPS):
            tap_wide[j, k] = jnp.broadcast_to(tap_rows[k : k + 1, 128 * j : 128 * j + 128], (8, 128))

    def groups(c, body, unroll=4):
        def one(i, _):
            body(pl.multiple_of(ROWS * c + GROUP * i, GROUP))
            return 0

        lax.fori_loop(0, ROWS // GROUP, one, 0, unroll=unroll)

    def normalize(c):
        x_load(c).wait()
        x_share(c).wait_recv()

        def body(first):
            rows = pl.ds(first, GROUP)
            a, b = xf[0, rows, :].astype(F32), xf[1, rows, :].astype(F32)
            mean = (jnp.sum(a, -1, keepdims=True) + jnp.sum(b, -1, keepdims=True)) / WIDTH
            a, b = a - mean, b - mean
            var = (jnp.sum(a * a, -1, keepdims=True) + jnp.sum(b * b, -1, keepdims=True)) / WIDTH
            scale = lax.rsqrt(var + epsilon)
            nb[rows, 0:HALF] = (a * scale).astype(BF16)
            nb[rows, HALF:WIDTH] = (b * scale).astype(BF16)
            rstd1[rows, :] = jnp.broadcast_to(scale, (GROUP, 128))

        groups(c, body)

    length = lengths[0]

    def valid_rows(first, count):
        position = lax.broadcasted_iota(jnp.int32, (count, 128), 0) + (seq * FRAMES + first)
        return jnp.where(position < length, 1.0, 0.0)

    def gate(c):
        for n in range(3):
            columns = slice(256 * n, 256 * n + 256)
            values = jnp.dot(nb[chunk(c), :], wv[:, columns], preferred_element_type=F32)
            sigma = sigmoid(jnp.dot(nb[chunk(c), :], wg[:, columns], preferred_element_type=F32))
            valid = valid_rows(ROWS * c, ROWS)
            vb[chunk(c), columns] = values
            sg[chunk(c), columns] = sigma
            for half in range(2):
                strip = slice(128 * half, 128 * half + 128)
                hidden = values[:, strip] * sigma[:, strip] * valid
                hb[2 * n + half, pl.ds(EDGE + ROWS * c, ROWS), :] = hidden.astype(BF16).astype(F32)

    def halo(buf, number):
        first, last = pl.ds(EDGE, EDGE), pl.ds(FRAMES, EDGE)
        before, after = pl.ds(0, EDGE), pl.ds(FRAMES + EDGE, EDGE)
        return (
            remote(buf.at[:, first], buf.at[:, after], halo_send.at[number], halo_recv.at[number], torus.beside(-1)),
            remote(buf.at[:, last], buf.at[:, before], halo_send.at[number + 1], halo_recv.at[number + 1], torus.beside(1)),
        )

    def halo_end(copies, buf):
        inside = (
            jnp.where(seq < 31, 1.0, 0.0).astype(F32),
            jnp.where(seq > 0, 1.0, 0.0).astype(F32),
        )
        for copy, keep, rows in zip(copies, inside, (pl.ds(FRAMES + EDGE, EDGE), pl.ds(0, EDGE))):
            copy.wait_recv()
            buf[:, rows, :] = buf[:, rows, :] * keep

    normalize(0)
    wv_load.wait()
    wg_load.wait()
    gate(0)
    normalize(2)
    gate(2)
    h_halo = halo(hb, 0)
    for copy in h_halo:
        copy.start()
    normalize(1)
    gate(1)

    def near(buf, j, row):
        return buf[j, pl.ds(row, 8), :]

    def convolve(buf, c, tap_at):
        def strip(j, _):
            def block(b, _):
                first = pl.multiple_of(ROWS * c + BLOCK * b, BLOCK)
                totals = [None] * (BLOCK // 8)
                for k in range(TAPS):
                    tap = tap_wide[j, tap_at(k)]
                    for i in range(BLOCK // 8):
                        term = near(buf, j, first + (EDGE - REACH + k + 8 * i)) * tap
                        totals[i] = term if k == 0 else totals[i] + term
                for i in range(BLOCK // 8):
                    cb[j, pl.ds(pl.multiple_of(first + 8 * i, 8), 8), :] = totals[i]
                return 0

            return lax.fori_loop(0, ROWS // BLOCK, block, 0)

        lax.fori_loop(0, 6, strip, 0)

    lane = lax.broadcasted_iota(jnp.int32, (GROUP, 128), 1)

    def stat_copy(number, c):
        at = 3 * number + c
        return remote(
            stat_out.at[number, chunk(c)], stat_in.at[number, chunk(c)], stat_send.at[at], stat_recv.at[at], partner
        )

    def put_stats(number, rows, first, second):
        stat_out[number, rows, :] = jnp.where(lane < 64, first, second)

    def get_stats(number, rows):
        total = (stat_out[number, rows, :] + stat_in[number, rows, :]) * (1.0 / WIDTH)
        return total[:, 0:1], total[:, 64:65]

    def conv_stats(c):
        def body(first):
            rows = pl.ds(first, GROUP)
            strips = [cb[j, rows, :] for j in range(6)]
            total, square = strips[0], strips[0] * strips[0]
            for strip in strips[1:]:
                total, square = total + strip, square + strip * strip
            put_stats(0, rows, jnp.sum(total, -1, keepdims=True), jnp.sum(square, -1, keepdims=True))

        groups(c, body)
        stat_copy(0, c).start()

    convolve(hb, 1, lambda k: k)
    conv_stats(1)
    u_load.wait()
    u_share.wait_recv()
    for load in wo_loads:
        load.wait()
    for c in range(CHUNKS):
        for n in range(3):
            ds[chunk(c), 256 * n : 256 * n + 256] = dot(
                uf[0, chunk(c), :], wo[0, 256 * n : 256 * n + 256, :], ((1,), (1,))
            ) + dot(uf[1, chunk(c), :], wo[1, 256 * n : 256 * n + 256, :], ((1,), (1,)))
    halo_end(h_halo, hb)
    for c in (0, 2):
        convolve(hb, c, lambda k: k)
        conv_stats(c)

    def activate(c):
        stat_copy(0, c).wait_recv()

        def body(first):
            rows = pl.ds(first, GROUP)
            mean, square = get_stats(0, rows)
            scale = lax.rsqrt(square - mean * mean + epsilon)
            rstd2[rows, :] = jnp.broadcast_to(scale, (GROUP, 128))
            total = cross = None
            for j in range(6):
                columns = slice(128 * j, 128 * j + 128)
                zhat = (cb[j, rows, :] - mean) * scale
                s = sigmoid(zhat)
                cb[j, rows, :] = zhat
                swish = zhat * s
                sw[rows, columns] = swish.astype(BF16)
                slope = ds[rows, columns] * (s + swish * (1.0 - s))
                ds[rows, columns] = slope
                total = slope if total is None else total + slope
                cross = slope * zhat if cross is None else cross + slope * zhat
            put_stats(1, rows, jnp.sum(total, -1, keepdims=True), jnp.sum(cross, -1, keepdims=True))

        groups(c, body)
        stat_copy(1, c).start()

    for c in (1, 0, 2):
        activate(c)

    def part_copy(number, c):
        at = 3 * number + c
        return remote(
            part_out.at[number, chunk(c)], part_in.at[number, chunk(c)], part_send.at[at], part_recv.at[at], partner
        )

    finals = (value_grad, gate_grad, out_grad)
    scatters = [
        [Scatter(torus, g, j, grads, landed, sums, finals, send, recv) for j in range(6)] for g in range(GRADS)
    ]

    def weight_grad(g, rows_of, right, n):
        for m in range(4):
            term = dot(rows_of(m), right[:, 256 * n : 256 * n + 256], ((0,), (0,)))
            for half in range(2):
                grads[g, 2 * n + half, m // 2, 2 * (m % 2) : 2 * (m % 2) + 2] = (
                    term[:, 128 * half : 128 * half + 128].reshape(2, 4, 2, 24, 128).astype(BF16)
                )
        for half in range(2):
            scatters[g][2 * n + half].begin(0)

    for n in range(3):
        weight_grad(2, lambda m: uf[m // 2, :, 384 * (m % 2) : 384 * (m % 2) + 384], sw, n)

    def conv_slope(c):
        stat_copy(1, c).wait_recv()

        def body(first):
            rows = pl.ds(first, GROUP)
            mean, cross = get_stats(1, rows)
            scale = rstd2[rows, :]
            for j in range(6):
                slope = scale * (ds[rows, 128 * j : 128 * j + 128] - mean - cb[j, rows, :] * cross)
                db[j, pl.ds(pl.multiple_of(first + EDGE, GROUP), GROUP), :] = slope.astype(BF16).astype(F32)

        groups(c, body)

    conv_slope(0)
    conv_slope(2)
    d_halo = halo(db, 2)
    for copy in d_halo:
        copy.start()
    conv_slope(1)

    def tap_terms(j):
        def block(b, totals):
            first = pl.multiple_of(BLOCK * b, BLOCK)
            slopes = [near(db, j, pl.multiple_of(first + (EDGE + 8 * i), 8)) for i in range(BLOCK // 8)]
            totals = list(totals)
            for m in range(BLOCK - 8 + TAPS):
                shifted = near(hb, j, first + (EDGE - REACH + m))
                for i in range(BLOCK // 8):
                    if 0 <= m - 8 * i < TAPS:
                        totals[m - 8 * i] = totals[m - 8 * i] + shifted * slopes[i]
            return tuple(totals)

        zeros = tuple(jnp.zeros((8, 128), F32) for _ in range(TAPS))
        totals = lax.fori_loop(0, FRAMES // BLOCK, block, zeros)
        for k in range(TAPS):
            tap_acc[j, k, :] = jnp.sum(totals[k], 0)
        tap_acc[j, TAPS, :] = jnp.zeros((128,), F32)

    tap_sums = [TapSum(torus, color, slots, tap_send, tap_recv) for color in range(3)]

    def tap_color(color):
        for j in (2 * color, 2 * color + 1):
            tap_terms(j)
        tap_sums[color].begin(0, tap_acc[2 * color : 2 * color + 2])

    def relay(g, phase):
        for one in scatters[g]:
            one.relay(phase)

    def finish(g, phase):
        for one in scatters[g]:
            one.finish(phase)
            if phase < 2:
                one.begin(phase + 1)

    def tap_step(phase):
        for color in range(3):
            total = tap_sums[color].finish(phase)
            if phase < 2:
                tap_sums[color].begin(phase + 1, total)
            else:
                for half in range(2):
                    j = 2 * color + half
                    taps_grad[:, 128 * j : 128 * j + 128] = total[half]


    def gate_slopes(c):
        def body(first):
            rows = pl.ds(first, GROUP)
            valid = valid_rows(first, GROUP)
            for j in range(6):
                columns = slice(128 * j, 128 * j + 128)
                sigma = sg[rows, columns]
                slope = cb[j, rows, :] * valid * sigma
                dv[rows, columns] = slope.astype(BF16)
                dg[rows, columns] = (slope * vb[rows, columns] * (1.0 - sigma)).astype(BF16)

        groups(c, body)

    convolve(db, 1, lambda k: TAPS - 1 - k)
    gate_slopes(1)
    relay(2, 0)
    halo_end(d_halo, db)
    for c in (0, 2):
        convolve(db, c, lambda k: TAPS - 1 - k)
        gate_slopes(c)
    finish(2, 0)

    for n in range(3):
        weight_grad(0, lambda m: nb[:, 384 * m : 384 * m + 384], dv, n)
    relay(2, 1)
    for n in range(3):
        weight_grad(1, lambda m: nb[:, 384 * m : 384 * m + 384], dg, n)

    def features(c, n, half):
        rows = pl.ds(pl.multiple_of(half * HALF + 256 * n, 256), 256)
        return dot(dv[chunk(c), :], wv[rows, :], ((1,), (1,))) + dot(dg[chunk(c), :], wg[rows, :], ((1,), (1,)))

    def features_over():
        for c in range(CHUNKS):
            for n in range(3):
                part_out[1, chunk(c), 256 * n : 256 * n + 256] = features(c, n, other).astype(BF16)
            part_copy(1, c).start()

    def features_here():
        for c in range(CHUNKS):
            for n in range(3):
                vb[chunk(c), 256 * n : 256 * n + 256] = features(c, n, me)

    def output_over():
        for c in range(CHUNKS):
            for n in range(3):
                part_out[0, chunk(c), 256 * n : 256 * n + 256] = jnp.dot(
                    sw[chunk(c), :], wo[other, :, 256 * n : 256 * n + 256], preferred_element_type=F32
                ).astype(BF16)
            part_copy(0, c).start()

    def output_here():
        for c in range(CHUNKS):
            for n in range(3):
                po[chunk(c), 256 * n : 256 * n + 256] = jnp.dot(
                    sw[chunk(c), :], wo[me, :, 256 * n : 256 * n + 256], preferred_element_type=F32
                )

    def output_rows(c):
        part_copy(0, c).wait_recv()

        def body(first):
            rows = pl.ds(first, GROUP)
            total = xf[me, rows, :].astype(F32) + (po[rows, :] + part_in[0, rows, :].astype(F32))
            xf[me, rows, :] = total.astype(BF16)

        groups(c, body)
        store = pltpu.make_async_copy(xf.at[me, chunk(c)], out.at[chunk(c)], store_sem.at[c])
        store.start()
        return store

    def feature_stats(c):
        part_copy(1, c).wait_recv()

        def body(first):
            rows = pl.ds(first, GROUP)
            slope = vb[rows, :] + part_in[1, rows, :].astype(F32)
            vb[rows, :] = slope
            unit = nb[rows, pl.ds(pl.multiple_of(me * HALF, HALF), HALF)].astype(F32)
            put_stats(2, rows, jnp.sum(slope, -1, keepdims=True), jnp.sum(slope * unit, -1, keepdims=True))

        groups(c, body)
        stat_copy(2, c).start()

    def input_rows(c):
        stat_copy(2, c).wait_recv()

        def body(first):
            rows = pl.ds(first, GROUP)
            mean, cross = get_stats(2, rows)
            scale = rstd1[rows, 0:1]
            unit = nb[rows, pl.ds(pl.multiple_of(me * HALF, HALF), HALF)].astype(F32)
            total = uf[me, rows, :].astype(F32) + scale * (vb[rows, :] - mean - unit * cross)
            uf[me, rows, :] = total.astype(BF16)

        groups(c, body)
        store = pltpu.make_async_copy(uf.at[me, chunk(c)], grad_in.at[chunk(c)], store_sem.at[3 + c])
        store.start()
        return store

    tap_color(0)
    relay(0, 0)
    tap_color(1)
    finish(2, 1)
    tap_color(2)
    relay(1, 0)
    relay(2, 2)
    features_over()
    finish(0, 0)
    tap_step(0)
    features_here()
    finish(1, 0)
    finish(2, 2)
    output_over()
    relay(0, 1)
    tap_step(1)
    output_here()
    relay(1, 1)
    for c in range(CHUNKS):
        feature_stats(c)
    finish(0, 1)
    tap_step(2)
    stores = [output_rows(c) for c in range(CHUNKS)]
    finish(1, 1)
    stores += [input_rows(c) for c in range(CHUNKS)]
    relay(0, 2)
    relay(1, 2)
    finish(0, 2)
    finish(1, 2)

    for group in scatters:
        for one in group:
            one.drain()
    for one in tap_sums:
        one.drain()
    for store in stores:
        store.wait()
    for copy in [x_share(c) for c in range(CHUNKS)] + [u_share]:
        copy.wait_send()
    for copy in h_halo + d_halo:
        copy.wait_send()
    for number in range(3):
        for c in range(CHUNKS):
            stat_copy(number, c).wait_send()
    for number in range(2):
        for c in range(CHUNKS):
            part_copy(number, c).wait_send()


def place_kernel(out, grad_in, value, gate, taps, outer, out_to, grad_in_to, value_to, gate_to, taps_to, outer_to, buf, load, store):
    def copies(source, target, n):
        found = []
        for c in range(CHUNKS):
            rows = pl.ds(ROWS * c, ROWS)
            found.append(
                (
                    pltpu.make_async_copy(source.at[rows], buf.at[n, rows], load.at[n, c]),
                    pltpu.make_async_copy(buf.at[n, rows], target.at[rows], store.at[n, c]),
                )
            )
        return found

    pairs = copies(out, out_to, 0) + copies(grad_in, grad_in_to, 1)
    for first, _ in pairs:
        first.start()
    value_to[...] = value[...]
    gate_to[...] = gate[...]
    taps_to[...] = taps[0:TAPS, :]
    outer_to[...] = outer[...]
    for first, second in pairs:
        first.wait()
        second.start()
    for _, second in pairs:
        second.wait()


def scratch_shapes():
    vmem, dma = pltpu.VMEM, pltpu.SemaphoreType.DMA
    shapes = [vmem((GRADS, 2, 3) + dims + (24, 128), BF16) for order in ORDERS for dims in LEFT[order]]
    shapes += [vmem((GRADS, 2) + dims + (24, 128), BF16) for order in ORDERS for dims in LEFT[order][:2]]
    copies = GRADS * 6 * 9
    shapes += [vmem((3, 3, 4, 2, 32, 128), F32), dma((copies,)), dma((copies,)), dma((27,)), dma((27,))]
    square, padded = (FRAMES, HALF), (6, FRAMES + 2 * EDGE, 128)
    shapes += [
        vmem((GRADS, 6, 2, 4, 4, 2, 24, 128), BF16),
        vmem((2,) + square, BF16),
        vmem((2,) + square, BF16),
        vmem((WIDTH, HALF), BF16),
        vmem((WIDTH, HALF), BF16),
        vmem((2,) + square, BF16),
        vmem((FRAMES, WIDTH), BF16),
        vmem((FRAMES, 128), F32),
        vmem(square, F32),
        vmem(square, F32),
        vmem(padded, F32),
        vmem(padded, F32),
        vmem((6, FRAMES, 128), F32),
        vmem(square, BF16),
        vmem(square, F32),
        vmem((FRAMES, 128), F32),
        vmem((3, FRAMES, 128), F32),
        vmem((3, FRAMES, 128), F32),
        vmem(square, BF16),
        vmem(square, BF16),
        vmem(square, F32),
        vmem((2,) + square, BF16),
        vmem((2,) + square, BF16),
        vmem((6, TAPS, 8, 128), F32),
        vmem((6, TAPS + 1, 128), F32),
        dma((8,)), dma((3,)), dma((3,)), dma(()), dma(()), dma((4,)), dma((4,)),
        dma((9,)), dma((9,)), dma((6,)), dma((6,)), dma((6,)),
    ]
    return shapes


def shards(inputs, lengths, cotangent, w_value, w_gate, kernel_taps, w_out):
    here, vmem = pl.BlockSpec(memory_space=pl.ANY), pl.BlockSpec(memory_space=pltpu.VMEM)
    smem = pl.BlockSpec(memory_space=pltpu.SMEM)
    rows = jax.ShapeDtypeStruct((FRAMES, HALF), BF16)
    block = jax.ShapeDtypeStruct((24, HALF), F32)
    output, input_gradient, value_grad, gate_grad, kernel_grad, out_grad = pl.pallas_call(
        kernel,
        out_shape=(rows, rows, block, block, jax.ShapeDtypeStruct((TAPS + 1, HALF), F32), block),
        in_specs=[smem, here, here, here, here, vmem, here],
        out_specs=(here, here, vmem, vmem, vmem, vmem),
        scratch_shapes=scratch_shapes(),
        compiler_params=pltpu.CompilerParams(
            collective_id=0, has_side_effects=True, vmem_limit_bytes=67043328
        ),
    )(lengths, inputs[0], cotangent[0], w_value, w_gate, kernel_taps, w_out)
    output, input_gradient, value_grad, gate_grad, kernel_grad, out_grad = pl.pallas_call(
        place_kernel,
        out_shape=(rows, rows, block, block, jax.ShapeDtypeStruct((TAPS, HALF), F32), block),
        in_specs=[here, here, vmem, vmem, vmem, vmem],
        out_specs=(here, here, vmem, vmem, vmem, vmem),
        scratch_shapes=[
            pltpu.VMEM((2, FRAMES, HALF), BF16),
            pltpu.SemaphoreType.DMA((2, CHUNKS)),
            pltpu.SemaphoreType.DMA((2, CHUNKS)),
        ],
    )(output, input_gradient, value_grad, gate_grad, kernel_grad, out_grad)
    return (output[None], input_gradient[None], value_grad, gate_grad, kernel_grad, out_grad.T)


def solution(mesh):
    return jax.shard_map(
        shards,
        mesh=mesh,
        in_specs=(
            P("dp", "seq", "tensor"),
            P("dp"),
            P("dp", "seq", "tensor"),
            P(None, "tensor"),
            P(None, "tensor"),
            P(None, "tensor"),
            P("tensor", None),
        ),
        out_specs=(
            P("dp", "seq", "tensor"),
            P("dp", "seq", "tensor"),
            P(("seq", "dp"), "tensor"),
            P(("seq", "dp"), "tensor"),
            P(None, "tensor"),
            P("tensor", ("seq", "dp")),
        ),
        check_vma=False,
    )
```

```python
import jax
import jax.numpy as jnp
from jax import lax
from jax.experimental import pallas as pl
from jax.experimental.pallas import tpu as pltpu
from jax.sharding import PartitionSpec as P

epsilon = 1e-05
MESH = pl.DeviceIdType.MESH
BF16, F32 = jnp.bfloat16, jnp.float32
ORDERS = ("xyz", "yzx", "zxy")
GRADS = 3
FRAMES, WIDTH, HALF = 768, 1536, 768
ROWS, CHUNKS = 256, 3
GROUP = 16
BLOCK = 32
TAPS, REACH, EDGE = 31, 15, 16
LEFT = {
    "xyz": ((4, 4), (4,), ()),
    "yzx": ((2, 4, 2), (2, 2), ()),
    "zxy": ((2, 4, 2), (4,), ()),
}


class Torus:
    def __init__(self):
        seq, low = lax.axis_index("seq"), lax.axis_index("dp")
        self.at = {
            "x": lax.div(seq, 16) * 2 + low,
            "y": lax.rem(seq, 4),
            "z": lax.rem(lax.div(seq, 4), 4),
        }

    def moved(self, axis, by):
        return lax.rem(self.at[axis] + (by + 4), 4)

    def beside(self, by):
        return {"seq": lax.rem(lax.axis_index("seq") + (by + 32), 32)}

    def peer(self, axis, by):
        at = dict(self.at)
        at[axis] = self.moved(axis, by)
        return {
            "seq": (lax.div(at["x"], 2) * 4 + at["z"]) * 4 + at["y"],
            "dp": lax.rem(at["x"], 2),
        }


def part_of(order, phase, coord):
    every = slice(None)
    high, low = lax.div(coord, 2), lax.rem(coord, 2)
    if phase == 0:
        return {
            "x": (high, every, every, low),
            "y": (every, every, coord, every),
            "z": (every, coord, every, every),
        }[order[0]]
    if phase == 1:
        return {"xyz": (every, coord), "yzx": (every, coord, every), "zxy": (high, every, low)}[order]
    return {"xyz": (coord,), "yzx": (high, low), "zxy": (coord,)}[order]


def wait_bytes(torus, ref, sem, sent=False):
    copy = pltpu.make_async_remote_copy(
        src_ref=ref, dst_ref=ref, send_sem=sem, recv_sem=sem, device_id=torus.peer("x", 1), device_id_type=MESH
    )
    if sent:
        copy.wait_send()
    else:
        copy.wait_recv()


class Scatter:
    def __init__(self, torus, grad, color, source, landed, sums, out, send, recv):
        self.torus, self.grad, self.color = torus, grad, color
        self.source, self.landed, self.sums, self.out = source, landed[color], sums[color], out
        self.sent, self.recv = send, recv
        self.order = ORDERS[color]

    def held(self, phase, half, by):
        part = part_of(self.order, phase, self.torus.moved(self.order[phase], by))
        if phase == 0:
            return self.source.at[(self.grad, 2 * self.color + half) + part]
        return self.sums[phase - 1].at[(self.grad, half) + part]

    def arrived(self, phase, late=1):
        return self.recv.at[(self.grad * 3 + self.color) * 4 + (late if phase == 0 else phase + 1)]

    def send(self, phase, half, which, ref, by):
        return pltpu.make_async_remote_copy(
            src_ref=ref,
            dst_ref=self.landed[phase].at[self.grad, half, which],
            send_sem=self.sent.at[self.color * 3 + phase],
            recv_sem=self.arrived(phase, 0 if which == 0 else 1),
            device_id=self.torus.peer(self.order[phase], by),
            device_id_type=MESH,
        )

    def begin(self, phase):
        for half, way in ((0, 1), (1, -1)):
            if phase == 0:
                self.send(0, half, 0, self.held(0, half, 2), way).start()
                self.send(0, half, 1, self.held(0, half, -way), -way).start()
            else:
                for which, by in enumerate((2, -way, way)):
                    self.send(phase, half, which, self.held(phase, half, by), by).start()

    def relay(self):
        wait_bytes(self.torus, self.landed[0].at[self.grad, :, 0], self.arrived(0, 0))
        for half, way in ((0, 1), (1, -1)):
            slot = self.landed[0].at[self.grad, half, 0]
            slot[...] = (slot[...].astype(F32) + self.held(0, half, way)[...].astype(F32)).astype(BF16)
            self.send(0, half, 2, slot, way).start()

    def finish(self, phase):
        first = 1 if phase == 0 else 0
        wait_bytes(self.torus, self.landed[phase].at[self.grad, :, first:3], self.arrived(phase))
        for half in range(2):
            total = self.held(phase, half, 0)[...].astype(F32)
            for which in range(first, 3):
                total = total + self.landed[phase][self.grad, half, which].astype(F32)
            if phase < 2:
                self.sums[phase][self.grad, half] = total.astype(BF16)
            else:
                strip = 2 * self.color + half
                self.out[self.grad][:, 128 * strip : 128 * strip + 128] = total
        if phase < 2:
            self.begin(phase + 1)


class TapSum:
    def __init__(self, torus, color, slots, send, recv):
        self.torus, self.color, self.slots, self.send, self.recv = torus, color, slots, send, recv
        self.order = ORDERS[color]

    def begin(self, phase, value):
        axis = self.order[phase]
        here = self.slots.at[self.color, phase, self.torus.at[axis]]
        here[...] = value.astype(BF16)
        for by in (1, 3, 2):
            pltpu.make_async_remote_copy(
                src_ref=here,
                dst_ref=here,
                send_sem=self.send,
                recv_sem=self.recv.at[self.color * 3 + phase],
                device_id=self.torus.peer(axis, by),
                device_id_type=MESH,
            ).start()

    def finish(self, phase):
        wait_bytes(self.torus, self.slots.at[self.color, phase, 0:3], self.recv.at[self.color * 3 + phase])
        slots = self.slots
        total = slots[self.color, phase, 0].astype(F32)
        for place in (1, 2, 3):
            total = total + slots[self.color, phase, place].astype(F32)
        return total


def greet(torus):
    barrier = pltpu.get_barrier_semaphore()
    peers = [torus.peer(axis, by) for axis in "xyz" for by in (1, 2, 3)]
    peers += [torus.beside(1), torus.beside(-1), {"tensor": 1 - lax.axis_index("tensor")}]
    for peer in peers:
        pl.semaphore_signal(barrier, inc=1, device_id=peer, device_id_type=MESH)
    pl.semaphore_wait(barrier, len(peers))


def sigmoid(values):
    return 0.5 * jnp.tanh(0.5 * values) + 0.5


def dot(a, b, contract):
    return lax.dot_general(a, b, (contract, ((), ())), preferred_element_type=F32)


def kernel(lengths, x, cot, w_value, w_gate, taps_in, w_out, out, grad_in, value_out, gate_out, taps_out, outer_out, *scratch):
    landed = [scratch[3 * c : 3 * c + 3] for c in range(3)]
    sums = [scratch[9 + 2 * c : 11 + 2 * c] for c in range(3)]
    (
        slots, send, recv, tap_send, tap_recv,
        grads, xf, uf, wv, wg, wo, nb, rstd1, vb, sg, hb, db, cb, sw, ds, rstd2, stat_out, stat_in,
        dv, dg, po, part_out, part_in, taps, length, tap_wide, tap_acc, value_grad, gate_grad, out_grad, taps_grad,
        load_sem, x_send, x_recv, u_send, u_recv, halo_send, halo_recv, stat_send, stat_recv, part_send, part_recv, store_sem,
    ) = scratch[15:]
    torus = Torus()
    me = lax.axis_index("tensor")
    other = 1 - me
    partner = {"tensor": other}
    seq = lax.axis_index("seq")

    def remote(src, dst, send_sem, recv_sem, to):
        return pltpu.make_async_remote_copy(
            src_ref=src, dst_ref=dst, send_sem=send_sem, recv_sem=recv_sem, device_id=to, device_id_type=MESH
        )

    def chunk(c):
        return pl.ds(ROWS * c, ROWS)

    def x_load(c):
        return pltpu.make_async_copy(x.at[chunk(c)], xf.at[me, chunk(c)], load_sem.at[c])

    def x_share(c):
        return remote(x.at[chunk(c)], xf.at[me, chunk(c)], x_send, x_recv.at[c], partner)

    tap_load = pltpu.make_async_copy(taps_in, taps, load_sem.at[8])
    length_load = pltpu.make_async_copy(lengths, length, load_sem.at[9])
    u_load = pltpu.make_async_copy(cot, uf.at[me], load_sem.at[3])
    u_share = remote(cot, uf.at[me], u_send, u_recv, partner)
    wv_load = pltpu.make_async_copy(w_value, wv, load_sem.at[4])
    wg_load = pltpu.make_async_copy(w_gate, wg, load_sem.at[5])
    wo_loads = [
        pltpu.make_async_copy(w_out.at[:, pl.ds(HALF * h, HALF)], wo.at[h], load_sem.at[6 + h])
        for h in range(2)
    ]
    for c in (0, 2, 1):
        x_load(c).start()
    tap_load.start()
    length_load.start()
    wv_load.start()
    wg_load.start()
    u_load.start()
    for load in wo_loads:
        load.start()
    greet(torus)
    for c in (0, 2, 1):
        x_share(c).start()
    u_share.start()

    tap_load.wait()
    length_load.wait()
    tap_rows = taps[...].astype(F32)
    for j in range(6):
        for k in range(TAPS):
            tap_wide[j, k] = jnp.broadcast_to(tap_rows[k : k + 1, 128 * j : 128 * j + 128], (8, 128))

    def groups(c, body, unroll=8):
        def one(i, _):
            body(pl.multiple_of(ROWS * c + GROUP * i, GROUP))
            return 0

        lax.fori_loop(0, ROWS // GROUP, one, 0, unroll=unroll)

    def normalize(c):
        x_load(c).wait()
        x_share(c).wait_recv()

        def body(first):
            rows = pl.ds(first, GROUP)
            a, b = xf[0, rows, :].astype(F32), xf[1, rows, :].astype(F32)
            mean = (jnp.sum(a, -1, keepdims=True) + jnp.sum(b, -1, keepdims=True)) / WIDTH
            a, b = a - mean, b - mean
            var = (jnp.sum(a * a, -1, keepdims=True) + jnp.sum(b * b, -1, keepdims=True)) / WIDTH
            scale = lax.rsqrt(var + epsilon)
            nb[rows, 0:HALF] = (a * scale).astype(BF16)
            nb[rows, HALF:WIDTH] = (b * scale).astype(BF16)
            rstd1[rows, :] = jnp.broadcast_to(scale, (GROUP, 128))

        groups(c, body)

    frames_valid = jnp.broadcast_to(length[...], (ROWS, 128))

    def valid_rows(first, count):
        position = lax.broadcasted_iota(jnp.int32, (count, 128), 0) + (seq * FRAMES + first)
        return jnp.where(position < frames_valid[0:count], 1.0, 0.0)

    def gate(c):
        for n in range(3):
            columns = slice(256 * n, 256 * n + 256)
            values = jnp.dot(nb[chunk(c), :], wv[:, columns], preferred_element_type=F32)
            sigma = sigmoid(jnp.dot(nb[chunk(c), :], wg[:, columns], preferred_element_type=F32))
            valid = valid_rows(ROWS * c, ROWS)
            vb[chunk(c), columns] = values
            sg[chunk(c), columns] = sigma
            for half in range(2):
                strip = slice(128 * half, 128 * half + 128)
                hidden = values[:, strip] * sigma[:, strip] * valid
                hb[2 * n + half, pl.ds(EDGE + ROWS * c, ROWS), :] = hidden.astype(BF16).astype(F32)

    def halo(buf, number):
        first, last = pl.ds(EDGE, EDGE), pl.ds(FRAMES, EDGE)
        before, after = pl.ds(0, EDGE), pl.ds(FRAMES + EDGE, EDGE)
        return (
            remote(buf.at[:, first], buf.at[:, after], halo_send, halo_recv.at[number], torus.beside(-1)),
            remote(buf.at[:, last], buf.at[:, before], halo_send, halo_recv.at[number + 1], torus.beside(1)),
        )

    def halo_end(copies, buf):
        inside = (
            jnp.where(seq < 31, 1.0, 0.0).astype(F32),
            jnp.where(seq > 0, 1.0, 0.0).astype(F32),
        )
        for copy, keep, rows in zip(copies, inside, (pl.ds(FRAMES + EDGE, EDGE), pl.ds(0, EDGE))):
            copy.wait_recv()
            buf[:, rows, :] = buf[:, rows, :] * keep

    normalize(0)
    wv_load.wait()
    wg_load.wait()
    gate(0)
    normalize(2)
    gate(2)
    h_halo = halo(hb, 0)
    for copy in h_halo:
        copy.start()
    normalize(1)
    gate(1)

    def near(buf, j, row):
        return buf[j, pl.ds(row, 8), :]

    def convolve(buf, c, tap_at, beside=None):
        def pair(p, _):
            if beside is not None:
                beside(c, p)
            for half in range(2):
                j = 2 * p + half
                for b in range(ROWS // BLOCK):
                    first = ROWS * c + BLOCK * b
                    totals = [None] * (BLOCK // 8)
                    for k in range(TAPS):
                        tap = tap_wide[j, tap_at(k)]
                        for i in range(BLOCK // 8):
                            term = near(buf, j, first + (EDGE - REACH + k + 8 * i)) * tap
                            totals[i] = term if k == 0 else totals[i] + term
                    for i in range(BLOCK // 8):
                        cb[j, pl.ds(first + 8 * i, 8), :] = totals[i]
            return 0

        lax.fori_loop(0, 3, pair, 0)

    def wide(p):
        return pl.ds(pl.multiple_of(256 * p, 256), 256)

    def slope_part(c, p):
        ds[chunk(c), wide(p)] = dot(uf[0, chunk(c), :], wo[0, wide(p), :], ((1,), (1,))) + dot(
            uf[1, chunk(c), :], wo[1, wide(p), :], ((1,), (1,))
        )

    def output_part(c, p):
        part_out[0, chunk(c), wide(p)] = jnp.dot(
            sw[chunk(c), :], wo[other, :, wide(p)], preferred_element_type=F32
        ).astype(BF16)
        po[chunk(c), wide(p)] = jnp.dot(sw[chunk(c), :], wo[me, :, wide(p)], preferred_element_type=F32)

    lane = lax.broadcasted_iota(jnp.int32, (GROUP, 128), 1)

    def stat_copy(number, c):
        at = 3 * number + c
        return remote(
            stat_out.at[number, chunk(c)], stat_in.at[number, chunk(c)], stat_send, stat_recv.at[at], partner
        )

    def put_stats(number, rows, first, second):
        stat_out[number, rows, :] = jnp.where(lane < 64, first, second)

    def get_stats(number, rows):
        total = (stat_out[number, rows, :] + stat_in[number, rows, :]) * (1.0 / WIDTH)
        return total[:, 0:1], total[:, 64:65]

    def conv_stats(c):
        def body(first):
            rows = pl.ds(first, GROUP)
            strips = [cb[j, rows, :] for j in range(6)]
            total, square = strips[0], strips[0] * strips[0]
            for strip in strips[1:]:
                total, square = total + strip, square + strip * strip
            put_stats(0, rows, jnp.sum(total, -1, keepdims=True), jnp.sum(square, -1, keepdims=True))

        groups(c, body)
        stat_copy(0, c).start()

    u_load.wait()
    u_share.wait_recv()
    for load in wo_loads:
        load.wait()
    convolve(hb, 1, lambda k: k, slope_part)
    conv_stats(1)
    halo_end(h_halo, hb)
    for c in (0, 2):
        convolve(hb, c, lambda k: k, slope_part)
        conv_stats(c)

    def store_small(n):
        source, target = ((value_grad, value_out), (gate_grad, gate_out), (out_grad, outer_out), (taps_grad, taps_out))[n]
        store = pltpu.make_async_copy(source, target, store_sem.at[2 + n])
        store.start()
        return store

    def activate(c):
        stat_copy(0, c).wait_recv()

        def body(first):
            rows = pl.ds(first, GROUP)
            mean, square = get_stats(0, rows)
            scale = lax.rsqrt(square - mean * mean + epsilon)
            rstd2[rows, :] = jnp.broadcast_to(scale, (GROUP, 128))
            total = cross = None
            for j in range(6):
                columns = slice(128 * j, 128 * j + 128)
                zhat = (cb[j, rows, :] - mean) * scale
                s = sigmoid(zhat)
                cb[j, rows, :] = zhat
                swish = zhat * s
                sw[rows, columns] = swish.astype(BF16)
                slope = ds[rows, columns] * (s + swish * (1.0 - s))
                ds[rows, columns] = slope
                total = slope if total is None else total + slope
                cross = slope * zhat if cross is None else cross + slope * zhat
            put_stats(1, rows, jnp.sum(total, -1, keepdims=True), jnp.sum(cross, -1, keepdims=True))

        groups(c, body)
        stat_copy(1, c).start()

    for c in (0, 2, 1):
        activate(c)

    def part_copy(number, c):
        at = 3 * number + c
        return remote(
            part_out.at[number, chunk(c)], part_in.at[number, chunk(c)], part_send, part_recv.at[at], partner
        )

    finals = (value_grad, gate_grad, out_grad)
    scatters = [
        [Scatter(torus, g, color, grads, landed, sums, finals, send, recv) for color in range(3)]
        for g in range(GRADS)
    ]

    def weight_grad(g, rows_of, right, n):
        for m in range(4):
            term = dot(rows_of(m), right[:, 256 * n : 256 * n + 256], ((0,), (0,)))
            for half in range(2):
                grads[g, 2 * n + half, m // 2, 2 * (m % 2) : 2 * (m % 2) + 2] = (
                    term[:, 128 * half : 128 * half + 128].reshape(2, 4, 2, 24, 128).astype(BF16)
                )
        scatters[g][n].begin(0)

    def conv_slope(c):
        stat_copy(1, c).wait_recv()

        def body(first):
            rows = pl.ds(first, GROUP)
            mean, cross = get_stats(1, rows)
            scale = rstd2[rows, :]
            for j in range(6):
                slope = scale * (ds[rows, 128 * j : 128 * j + 128] - mean - cb[j, rows, :] * cross)
                db[j, pl.ds(pl.multiple_of(first + EDGE, GROUP), GROUP), :] = slope.astype(BF16).astype(F32)

        groups(c, body)

    conv_slope(0)
    conv_slope(2)
    d_halo = halo(db, 2)
    for copy in d_halo:
        copy.start()
    conv_slope(1)
    for n in range(3):
        weight_grad(2, lambda m: uf[m // 2, :, 384 * (m % 2) : 384 * (m % 2) + 384], sw, n)

    def tap_terms(j):
        def block(b, totals):
            first = pl.multiple_of(BLOCK * b, BLOCK)
            slopes = [near(db, j, pl.multiple_of(first + (EDGE + 8 * i), 8)) for i in range(BLOCK // 8)]
            totals = list(totals)
            for m in range(BLOCK - 8 + TAPS):
                shifted = near(hb, j, first + (EDGE - REACH + m))
                for i in range(BLOCK // 8):
                    if 0 <= m - 8 * i < TAPS:
                        totals[m - 8 * i] = totals[m - 8 * i] + shifted * slopes[i]
            return tuple(totals)

        zeros = tuple(jnp.zeros((8, 128), F32) for _ in range(TAPS))
        totals = lax.fori_loop(0, FRAMES // BLOCK, block, zeros)
        for k in range(TAPS):
            tap_acc[j, k, :] = jnp.sum(totals[k], 0)
        tap_acc[j, TAPS, :] = jnp.zeros((128,), F32)

    tap_sums = [TapSum(torus, color, slots, tap_send, tap_recv) for color in range(3)]

    def tap_color(color):
        tap_sums[color].begin(0, tap_acc[2 * color : 2 * color + 2])

    def relay(g, colors=(0, 1, 2)):
        for color in colors:
            scatters[g][color].relay()

    def finish(g, phase, colors=(0, 1, 2)):
        for color in colors:
            scatters[g][color].finish(phase)

    def tap_step(phase, color):
        total = tap_sums[color].finish(phase)
        if phase < 2:
            tap_sums[color].begin(phase + 1, total)
        else:
            for half in range(2):
                j = 2 * color + half
                taps_grad[:, 128 * j : 128 * j + 128] = total[half, 0:TAPS, :]

    def gate_slopes(c):
        def body(first):
            rows = pl.ds(first, GROUP)
            valid = valid_rows(first, GROUP)
            for j in range(6):
                columns = slice(128 * j, 128 * j + 128)
                sigma = sg[rows, columns]
                slope = cb[j, rows, :] * valid * sigma
                dv[rows, columns] = slope.astype(BF16)
                dg[rows, columns] = (slope * vb[rows, columns] * (1.0 - sigma)).astype(BF16)

        groups(c, body)

    convolve(db, 1, lambda k: TAPS - 1 - k, output_part)
    part_copy(0, 1).start()
    gate_slopes(1)
    halo_end(d_halo, db)
    convolve(db, 0, lambda k: TAPS - 1 - k, output_part)
    part_copy(0, 0).start()
    gate_slopes(0)
    relay(2, (0,))
    convolve(db, 2, lambda k: TAPS - 1 - k, output_part)
    part_copy(0, 2).start()
    gate_slopes(2)

    for n in range(3):
        weight_grad(0, lambda m: nb[:, 384 * m : 384 * m + 384], dv, n)
    relay(2, (1, 2))
    for n in range(3):
        weight_grad(1, lambda m: nb[:, 384 * m : 384 * m + 384], dg, n)

    def features(c, n, half):
        rows = pl.ds(pl.multiple_of(half * HALF + 256 * n, 256), 256)
        return dot(dv[chunk(c), :], wv[rows, :], ((1,), (1,))) + dot(dg[chunk(c), :], wg[rows, :], ((1,), (1,)))

    def features_over(c):
        for n in range(3):
            part_out[1, chunk(c), 256 * n : 256 * n + 256] = features(c, n, other).astype(BF16)
        part_copy(1, c).start()

    def features_here(c):
        for n in range(3):
            vb[chunk(c), 256 * n : 256 * n + 256] = features(c, n, me)

    def output_rows(c):
        part_copy(0, c).wait_recv()

        def body(first):
            rows = pl.ds(first, GROUP)
            total = xf[me, rows, :].astype(F32) + (po[rows, :] + part_in[0, rows, :].astype(F32))
            xf[me, rows, :] = total.astype(BF16)

        groups(c, body)
        store = pltpu.make_async_copy(xf.at[me, chunk(c)], out.at[chunk(c)], store_sem.at[0])
        store.start()

    def feature_stats(c):
        part_copy(1, c).wait_recv()

        def body(first):
            rows = pl.ds(first, GROUP)
            slope = vb[rows, :] + part_in[1, rows, :].astype(F32)
            vb[rows, :] = slope
            unit = nb[rows, pl.ds(pl.multiple_of(me * HALF, HALF), HALF)].astype(F32)
            put_stats(2, rows, jnp.sum(slope, -1, keepdims=True), jnp.sum(slope * unit, -1, keepdims=True))

        groups(c, body)
        stat_copy(2, c).start()

    def input_rows(c):
        stat_copy(2, c).wait_recv()

        def body(first):
            rows = pl.ds(first, GROUP)
            mean, cross = get_stats(2, rows)
            scale = rstd1[rows, 0:1]
            unit = nb[rows, pl.ds(pl.multiple_of(me * HALF, HALF), HALF)].astype(F32)
            total = uf[me, rows, :].astype(F32) + scale * (vb[rows, :] - mean - unit * cross)
            uf[me, rows, :] = total.astype(BF16)

        groups(c, body)
        store = pltpu.make_async_copy(uf.at[me, chunk(c)], grad_in.at[chunk(c)], store_sem.at[1])
        store.start()

    tap_terms(0)
    tap_terms(1)
    tap_color(0)
    relay(0, (0,))
    tap_terms(2)
    relay(0, (1,))
    finish(2, 0, (0,))
    tap_terms(3)
    tap_color(1)
    finish(2, 0, (1,))
    tap_terms(4)
    relay(0, (2,))
    finish(2, 0, (2,))
    tap_terms(5)
    tap_color(2)
    features_over(0)
    relay(1, (0,))
    tap_step(0, 0)
    features_over(1)
    relay(1, (1,))
    features_over(2)
    relay(1, (2,))
    finish(0, 0, (0,))
    tap_step(0, 1)
    features_here(0)
    finish(0, 0, (1,))
    tap_step(1, 0)
    features_here(1)
    finish(0, 0, (2,))
    finish(1, 0, (0,))
    finish(2, 1)
    features_here(2)
    finish(1, 0, (1,))
    tap_step(0, 2)
    for c in range(CHUNKS):
        feature_stats(c)
    finish(1, 0, (2,))
    tap_step(1, 1)
    finish(0, 1)
    for c in range(CHUNKS):
        output_rows(c)
    tap_step(2, 0)
    for c in range(CHUNKS):
        input_rows(c)
    finish(2, 2)
    stores = [store_small(2)]
    finish(1, 1)
    tap_step(1, 2)
    tap_step(2, 1)
    finish(0, 2)
    stores.append(store_small(0))
    finish(1, 2)
    stores.append(store_small(1))
    tap_step(2, 2)
    stores.append(store_small(3))

    for color in range(3):
        for phase in range(3):
            wait_bytes(torus, landed[color][phase], send.at[color * 3 + phase], sent=True)
    wait_bytes(torus, slots.at[:, :, 0:3], tap_send, sent=True)
    wait_bytes(torus, xf.at[me], x_send, sent=True)
    wait_bytes(torus, uf.at[me], u_send, sent=True)
    wait_bytes(torus, hb.at[:, 0 : 4 * EDGE], halo_send, sent=True)
    wait_bytes(torus, stat_out, stat_send, sent=True)
    wait_bytes(torus, part_out, part_send, sent=True)
    pltpu.make_async_copy(xf.at[me], out, store_sem.at[0]).wait()
    pltpu.make_async_copy(uf.at[me], grad_in, store_sem.at[1]).wait()
    for store in stores:
        store.wait()


def place_kernel(*refs):
    sources, targets, held, (load, store) = refs[:6], refs[6:12], refs[12:18], refs[18:]
    parts = [(n, slice(None)) for n in range(2, 6)]
    parts += [(n, pl.ds(ROWS * c, ROWS)) for n in range(2) for c in range(CHUNKS)]
    pairs = [
        (
            pltpu.make_async_copy(sources[n].at[rows], held[n].at[rows], load.at[at]),
            pltpu.make_async_copy(held[n].at[rows], targets[n].at[rows], store.at[at]),
        )
        for at, (n, rows) in enumerate(parts)
    ]
    for first, _ in pairs:
        first.start()
    for first, second in pairs:
        first.wait()
        second.start()
    for _, second in pairs:
        second.wait()


def scratch_shapes():
    vmem, dma = pltpu.VMEM, pltpu.SemaphoreType.DMA
    shapes = [vmem((GRADS, 2, 3) + dims + (24, 128), BF16) for order in ORDERS for dims in LEFT[order]]
    shapes += [vmem((GRADS, 2) + dims + (24, 128), BF16) for order in ORDERS for dims in LEFT[order][:2]]
    shapes += [vmem((3, 3, 4, 2, 32, 128), BF16), dma((9,)), dma((GRADS * 3 * 4,)), dma(()), dma((9,))]
    square, padded = (FRAMES, HALF), (6, FRAMES + 2 * EDGE, 128)
    shapes += [
        vmem((GRADS, 6, 2, 4, 4, 2, 24, 128), BF16),
        vmem((2,) + square, BF16),
        vmem((2,) + square, BF16),
        vmem((WIDTH, HALF), BF16),
        vmem((WIDTH, HALF), BF16),
        vmem((2,) + square, BF16),
        vmem((FRAMES, WIDTH), BF16),
        vmem((FRAMES, 128), F32),
        vmem(square, F32),
        vmem(square, F32),
        vmem(padded, F32),
        vmem(padded, F32),
        vmem((6, FRAMES, 128), F32),
        vmem(square, BF16),
        vmem(square, F32),
        vmem((FRAMES, 128), F32),
        vmem((3, FRAMES, 128), F32),
        vmem((3, FRAMES, 128), F32),
        vmem(square, BF16),
        vmem(square, BF16),
        vmem(square, F32),
        vmem((2,) + square, BF16),
        vmem((2,) + square, BF16),
        vmem((TAPS, HALF), BF16),
        vmem((1, 1), jnp.int32),
        vmem((6, TAPS, 8, 128), F32),
        vmem((6, TAPS + 1, 128), F32),
        vmem((24, HALF), F32), vmem((24, HALF), F32), vmem((24, HALF), F32), vmem((TAPS, HALF), F32),
        dma((10,)), dma(()), dma((3,)), dma(()), dma(()), dma(()), dma((4,)),
        dma(()), dma((9,)), dma(()), dma((6,)), dma((6,)),
    ]
    return shapes


def shards(inputs, lengths, cotangent, w_value, w_gate, kernel_taps, w_out):
    here = pl.BlockSpec(memory_space=pl.ANY)
    rows = jax.ShapeDtypeStruct((FRAMES, HALF), BF16)
    block = jax.ShapeDtypeStruct((24, HALF), F32)
    results = (rows, rows, block, block, jax.ShapeDtypeStruct((TAPS, HALF), F32), block)
    output, input_gradient, value_grad, gate_grad, kernel_grad, out_grad = pl.pallas_call(
        kernel,
        out_shape=results,
        in_specs=[here] * 7,
        out_specs=(here,) * 6,
        scratch_shapes=scratch_shapes(),
        compiler_params=pltpu.CompilerParams(
            collective_id=0, has_side_effects=True, vmem_limit_bytes=67043328
        ),
    )(lengths.reshape(1, 1), inputs[0], cotangent[0], w_value, w_gate, kernel_taps, w_out)
    output, input_gradient, value_grad, gate_grad, kernel_grad, out_grad = pl.pallas_call(
        place_kernel,
        out_shape=results,
        in_specs=[here] * 6,
        out_specs=(here,) * 6,
        scratch_shapes=[pltpu.VMEM(result.shape, result.dtype) for result in results]
        + [pltpu.SemaphoreType.DMA((10,)), pltpu.SemaphoreType.DMA((10,))],
    )(output, input_gradient, value_grad, gate_grad, kernel_grad, out_grad)
    return (output[None], input_gradient[None], value_grad, gate_grad, kernel_grad, out_grad.T)


def solution(mesh):
    return jax.shard_map(
        shards,
        mesh=mesh,
        in_specs=(
            P("dp", "seq", "tensor"),
            P("dp"),
            P("dp", "seq", "tensor"),
            P(None, "tensor"),
            P(None, "tensor"),
            P(None, "tensor"),
            P("tensor", None),
        ),
        out_specs=(
            P("dp", "seq", "tensor"),
            P("dp", "seq", "tensor"),
            P(("seq", "dp"), "tensor"),
            P(("seq", "dp"), "tensor"),
            P(None, "tensor"),
            P("tensor", ("seq", "dp")),
        ),
        check_vma=False,
    )
```

```python
import jax
import jax.numpy as jnp
from jax import lax
from jax.experimental import pallas as pl
from jax.experimental.pallas import tpu as pltpu
from jax.sharding import PartitionSpec as P

epsilon = 1e-05
MESH = pl.DeviceIdType.MESH
BF16, F32 = jnp.bfloat16, jnp.float32
ORDERS = ("xyz", "yzx", "zxy")
GRADS = 3
FRAMES, WIDTH, HALF = 768, 1536, 768
ROWS, CHUNKS = 256, 3
GROUP = 16
BLOCK = 32
TAPS, REACH, EDGE = 31, 15, 16
LEFT = {
    "xyz": ((4, 4), (4,), ()),
    "yzx": ((2, 4, 2), (2, 2), ()),
    "zxy": ((2, 4, 2), (4,), ()),
}


class Torus:
    def __init__(self):
        seq, low = lax.axis_index("seq"), lax.axis_index("dp")
        self.at = {
            "x": lax.div(seq, 16) * 2 + low,
            "y": lax.rem(seq, 4),
            "z": lax.rem(lax.div(seq, 4), 4),
        }

    def moved(self, axis, by):
        return lax.rem(self.at[axis] + (by + 4), 4)

    def beside(self, by):
        return {"seq": lax.rem(lax.axis_index("seq") + (by + 32), 32)}

    def peer(self, axis, by):
        at = dict(self.at)
        at[axis] = self.moved(axis, by)
        return {
            "seq": (lax.div(at["x"], 2) * 4 + at["z"]) * 4 + at["y"],
            "dp": lax.rem(at["x"], 2),
        }


def part_of(order, phase, coord):
    every = slice(None)
    high, low = lax.div(coord, 2), lax.rem(coord, 2)
    if phase == 0:
        return {
            "x": (high, every, every, low),
            "y": (every, every, coord, every),
            "z": (every, coord, every, every),
        }[order[0]]
    if phase == 1:
        return {"xyz": (every, coord), "yzx": (every, coord, every), "zxy": (high, every, low)}[order]
    return {"xyz": (coord,), "yzx": (high, low), "zxy": (coord,)}[order]


def wait_bytes(torus, ref, sem, sent=False):
    copy = pltpu.make_async_remote_copy(
        src_ref=ref, dst_ref=ref, send_sem=sem, recv_sem=sem, device_id=torus.peer("x", 1), device_id_type=MESH
    )
    if sent:
        copy.wait_send()
    else:
        copy.wait_recv()


class Scatter:
    def __init__(self, torus, grad, color, source, landed, sums, out, send, recv):
        self.torus, self.grad, self.color = torus, grad, color
        self.source, self.landed, self.sums, self.out = source, landed[color], sums[color], out
        self.sent, self.recv = send, recv
        self.order = ORDERS[color]

    def held(self, phase, half, by):
        part = part_of(self.order, phase, self.torus.moved(self.order[phase], by))
        if phase == 0:
            return self.source.at[(self.grad, 2 * self.color + half) + part]
        return self.sums[phase - 1].at[(self.grad, half) + part]

    def arrived(self, phase, late=1):
        return self.recv.at[(self.grad * 3 + self.color) * 4 + (late if phase == 0 else phase + 1)]

    def send(self, phase, half, which, ref, by):
        return pltpu.make_async_remote_copy(
            src_ref=ref,
            dst_ref=self.landed[phase].at[self.grad, half, which],
            send_sem=self.sent.at[self.color * 3 + phase],
            recv_sem=self.arrived(phase, 0 if which == 0 else 1),
            device_id=self.torus.peer(self.order[phase], by),
            device_id_type=MESH,
        )

    def begin(self, phase):
        for half, way in ((0, 1), (1, -1)):
            if phase == 0:
                self.send(0, half, 0, self.held(0, half, 2), way).start()
            else:
                for which, by in enumerate((2, -way, way)):
                    self.send(phase, half, which, self.held(phase, half, by), by).start()

    def straight(self):
        for half, way in ((0, 1), (1, -1)):
            self.send(0, half, 1, self.held(0, half, -way), -way).start()

    def relay(self):
        wait_bytes(self.torus, self.landed[0].at[self.grad, :, 0], self.arrived(0, 0))
        for half, way in ((0, 1), (1, -1)):
            slot = self.landed[0].at[self.grad, half, 0]
            slot[...] = (slot[...].astype(F32) + self.held(0, half, way)[...].astype(F32)).astype(BF16)
            self.send(0, half, 2, slot, way).start()

    def finish(self, phase):
        first = 1 if phase == 0 else 0
        wait_bytes(self.torus, self.landed[phase].at[self.grad, :, first:3], self.arrived(phase))
        for half in range(2):
            total = self.held(phase, half, 0)[...].astype(F32)
            for which in range(first, 3):
                total = total + self.landed[phase][self.grad, half, which].astype(F32)
            if phase < 2:
                self.sums[phase][self.grad, half] = total.astype(BF16)
            else:
                strip = 2 * self.color + half
                self.out[self.grad][:, 128 * strip : 128 * strip + 128] = total
        if phase < 2:
            self.begin(phase + 1)


class TapSum:
    def __init__(self, torus, color, slots, send, recv):
        self.torus, self.color, self.slots, self.send, self.recv = torus, color, slots, send, recv
        self.order = ORDERS[color]

    def begin(self, phase, value):
        axis = self.order[phase]
        here = self.slots.at[self.color, phase, self.torus.at[axis]]
        here[...] = value.astype(BF16)
        for by in (1, 3, 2):
            pltpu.make_async_remote_copy(
                src_ref=here,
                dst_ref=here,
                send_sem=self.send,
                recv_sem=self.recv.at[self.color * 3 + phase],
                device_id=self.torus.peer(axis, by),
                device_id_type=MESH,
            ).start()

    def finish(self, phase):
        wait_bytes(self.torus, self.slots.at[self.color, phase, 0:3], self.recv.at[self.color * 3 + phase])
        slots = self.slots
        total = slots[self.color, phase, 0].astype(F32)
        for place in (1, 2, 3):
            total = total + slots[self.color, phase, place].astype(F32)
        return total


def greet(torus):
    barrier = pltpu.get_barrier_semaphore()
    peers = [torus.peer(axis, by) for axis in "xyz" for by in (1, 2, 3)]
    peers += [torus.beside(1), torus.beside(-1), {"tensor": 1 - lax.axis_index("tensor")}]
    for peer in peers:
        pl.semaphore_signal(barrier, inc=1, device_id=peer, device_id_type=MESH)
    pl.semaphore_wait(barrier, len(peers))


def sigmoid(values):
    return 0.5 * jnp.tanh(0.5 * values) + 0.5


def dot(a, b, contract):
    return lax.dot_general(a, b, (contract, ((), ())), preferred_element_type=F32)


def kernel(lengths, x, cot, w_value, w_gate, taps_in, w_out, out, grad_in, value_out, gate_out, taps_out, outer_out, *scratch):
    landed = [scratch[3 * c : 3 * c + 3] for c in range(3)]
    sums = [scratch[9 + 2 * c : 11 + 2 * c] for c in range(3)]
    (
        slots, send, recv, tap_send, tap_recv,
        grads, xf, uf, wv, wg, wo, nb, rstd1, vb, sg, hb, db, cb, sw, ds, rstd2, stat_out, stat_in,
        dv, dg, po, part_out, part_in, taps, length, tap_wide, tap_acc, value_grad, gate_grad, out_grad, taps_grad,
        load_sem, x_send, x_recv, u_send, u_recv, halo_send, halo_recv, stat_send, stat_recv, part_send, part_recv, store_sem,
    ) = scratch[15:]
    torus = Torus()
    me = lax.axis_index("tensor")
    other = 1 - me
    partner = {"tensor": other}
    seq = lax.axis_index("seq")

    def remote(src, dst, send_sem, recv_sem, to):
        return pltpu.make_async_remote_copy(
            src_ref=src, dst_ref=dst, send_sem=send_sem, recv_sem=recv_sem, device_id=to, device_id_type=MESH
        )

    def chunk(c):
        return pl.ds(ROWS * c, ROWS)

    def x_load(c):
        return pltpu.make_async_copy(x.at[chunk(c)], xf.at[me, chunk(c)], load_sem.at[c])

    def x_share(c):
        return remote(x.at[chunk(c)], xf.at[me, chunk(c)], x_send, x_recv.at[c], partner)

    tap_load = pltpu.make_async_copy(taps_in, taps, load_sem.at[8])
    length_load = pltpu.make_async_copy(lengths, length, load_sem.at[9])
    u_load = pltpu.make_async_copy(cot, uf.at[me], load_sem.at[3])
    u_share = remote(cot, uf.at[me], u_send, u_recv, partner)
    wv_load = pltpu.make_async_copy(w_value, wv, load_sem.at[4])
    wg_load = pltpu.make_async_copy(w_gate, wg, load_sem.at[5])
    wo_loads = [
        pltpu.make_async_copy(w_out.at[:, pl.ds(HALF * h, HALF)], wo.at[h], load_sem.at[6 + h])
        for h in range(2)
    ]
    for c in (0, 2, 1):
        x_load(c).start()
    tap_load.start()
    length_load.start()
    greet(torus)
    for c in (0, 2, 1):
        x_share(c).start()
    wv_load.start()
    wg_load.start()
    u_load.start()
    u_share.start()
    for load in wo_loads:
        load.start()

    tap_load.wait()
    length_load.wait()
    tap_rows = taps[...].astype(F32)
    for j in range(6):
        for k in range(TAPS):
            tap_wide[j, k] = jnp.broadcast_to(tap_rows[k : k + 1, 128 * j : 128 * j + 128], (8, 128))

    def groups(c, body, unroll=8):
        def one(i, _):
            body(pl.multiple_of(ROWS * c + GROUP * i, GROUP))
            return 0

        lax.fori_loop(0, ROWS // GROUP, one, 0, unroll=unroll)

    def normalize(c):
        x_load(c).wait()
        x_share(c).wait_recv()

        def body(first):
            rows = pl.ds(first, GROUP)
            a, b = xf[0, rows, :].astype(F32), xf[1, rows, :].astype(F32)
            mean = (jnp.sum(a, -1, keepdims=True) + jnp.sum(b, -1, keepdims=True)) / WIDTH
            a, b = a - mean, b - mean
            var = (jnp.sum(a * a, -1, keepdims=True) + jnp.sum(b * b, -1, keepdims=True)) / WIDTH
            scale = lax.rsqrt(var + epsilon)
            nb[rows, 0:HALF] = (a * scale).astype(BF16)
            nb[rows, HALF:WIDTH] = (b * scale).astype(BF16)
            rstd1[rows, :] = jnp.broadcast_to(scale, (GROUP, 128))

        groups(c, body)

    frames_valid = jnp.broadcast_to(length[...], (ROWS, 128))

    def valid_rows(first, count):
        position = lax.broadcasted_iota(jnp.int32, (count, 128), 0) + (seq * FRAMES + first)
        return jnp.where(position < frames_valid[0:count], 1.0, 0.0)

    def gate(c):
        for n in range(3):
            columns = slice(256 * n, 256 * n + 256)
            values = jnp.dot(nb[chunk(c), :], wv[:, columns], preferred_element_type=F32)
            sigma = sigmoid(jnp.dot(nb[chunk(c), :], wg[:, columns], preferred_element_type=F32))
            valid = valid_rows(ROWS * c, ROWS)
            vb[chunk(c), columns] = values
            sg[chunk(c), columns] = sigma
            for half in range(2):
                strip = slice(128 * half, 128 * half + 128)
                hidden = values[:, strip] * sigma[:, strip] * valid
                hb[2 * n + half, pl.ds(EDGE + ROWS * c, ROWS), :] = hidden.astype(BF16).astype(F32)

    def halo(buf, number):
        first, last = pl.ds(EDGE, EDGE), pl.ds(FRAMES, EDGE)
        before, after = pl.ds(0, EDGE), pl.ds(FRAMES + EDGE, EDGE)
        return (
            remote(buf.at[:, first], buf.at[:, after], halo_send, halo_recv.at[number], torus.beside(-1)),
            remote(buf.at[:, last], buf.at[:, before], halo_send, halo_recv.at[number + 1], torus.beside(1)),
        )

    def halo_end(copies, buf):
        inside = (
            jnp.where(seq < 31, 1.0, 0.0).astype(F32),
            jnp.where(seq > 0, 1.0, 0.0).astype(F32),
        )
        for copy, keep, rows in zip(copies, inside, (pl.ds(FRAMES + EDGE, EDGE), pl.ds(0, EDGE))):
            copy.wait_recv()
            buf[:, rows, :] = buf[:, rows, :] * keep

    normalize(0)
    wv_load.wait()
    wg_load.wait()
    gate(0)
    normalize(2)
    gate(2)
    h_halo = halo(hb, 0)
    for copy in h_halo:
        copy.start()
    normalize(1)
    gate(1)

    def near(buf, j, row):
        return buf[j, pl.ds(row, 8), :]

    def convolve(buf, c, tap_at, beside=None):
        def pair(p, _):
            if beside is not None:
                beside(c, p)
            for half in range(2):
                j = 2 * p + half
                for b in range(ROWS // BLOCK):
                    first = ROWS * c + BLOCK * b
                    totals = [None] * (BLOCK // 8)
                    for k in range(TAPS):
                        tap = tap_wide[j, tap_at(k)]
                        for i in range(BLOCK // 8):
                            term = near(buf, j, first + (EDGE - REACH + k + 8 * i)) * tap
                            totals[i] = term if k == 0 else totals[i] + term
                    for i in range(BLOCK // 8):
                        cb[j, pl.ds(first + 8 * i, 8), :] = totals[i]
            return 0

        lax.fori_loop(0, 3, pair, 0)

    def wide(p):
        return pl.ds(pl.multiple_of(256 * p, 256), 256)

    def slope_part(c, p):
        ds[chunk(c), wide(p)] = dot(uf[0, chunk(c), :], wo[0, wide(p), :], ((1,), (1,))) + dot(
            uf[1, chunk(c), :], wo[1, wide(p), :], ((1,), (1,))
        )

    def output_part(c, p):
        part_out[0, chunk(c), wide(p)] = jnp.dot(
            sw[chunk(c), :], wo[other, :, wide(p)], preferred_element_type=F32
        ).astype(BF16)
        po[chunk(c), wide(p)] = jnp.dot(sw[chunk(c), :], wo[me, :, wide(p)], preferred_element_type=F32)

    lane = lax.broadcasted_iota(jnp.int32, (GROUP, 128), 1)

    def stat_copy(number, c):
        at = 3 * number + c
        return remote(
            stat_out.at[number, chunk(c)], stat_in.at[number, chunk(c)], stat_send, stat_recv.at[at], partner
        )

    def put_stats(number, rows, first, second):
        stat_out[number, rows, :] = jnp.where(lane < 64, first, second)

    def get_stats(number, rows):
        total = (stat_out[number, rows, :] + stat_in[number, rows, :]) * (1.0 / WIDTH)
        return total[:, 0:1], total[:, 64:65]

    def conv_stats(c):
        def body(first):
            rows = pl.ds(first, GROUP)
            strips = [cb[j, rows, :] for j in range(6)]
            total, square = strips[0], strips[0] * strips[0]
            for strip in strips[1:]:
                total, square = total + strip, square + strip * strip
            put_stats(0, rows, jnp.sum(total, -1, keepdims=True), jnp.sum(square, -1, keepdims=True))

        groups(c, body)
        stat_copy(0, c).start()

    u_load.wait()
    u_share.wait_recv()
    for load in wo_loads:
        load.wait()
    convolve(hb, 1, lambda k: k, slope_part)
    conv_stats(1)
    halo_end(h_halo, hb)
    for c in (0, 2):
        convolve(hb, c, lambda k: k, slope_part)
        conv_stats(c)

    def store_small(n):
        source, target = ((value_grad, value_out), (gate_grad, gate_out), (out_grad, outer_out), (taps_grad, taps_out))[n]
        store = pltpu.make_async_copy(source, target, store_sem.at[2 + n])
        store.start()
        return store

    def activate(c):
        stat_copy(0, c).wait_recv()

        def body(first):
            rows = pl.ds(first, GROUP)
            mean, square = get_stats(0, rows)
            scale = lax.rsqrt(square - mean * mean + epsilon)
            rstd2[rows, :] = jnp.broadcast_to(scale, (GROUP, 128))
            total = cross = None
            for j in range(6):
                columns = slice(128 * j, 128 * j + 128)
                zhat = (cb[j, rows, :] - mean) * scale
                s = sigmoid(zhat)
                cb[j, rows, :] = zhat
                swish = zhat * s
                sw[rows, columns] = swish.astype(BF16)
                slope = ds[rows, columns] * (s + swish * (1.0 - s))
                ds[rows, columns] = slope
                total = slope if total is None else total + slope
                cross = slope * zhat if cross is None else cross + slope * zhat
            put_stats(1, rows, jnp.sum(total, -1, keepdims=True), jnp.sum(cross, -1, keepdims=True))

        groups(c, body)
        stat_copy(1, c).start()

    for c in (0, 2, 1):
        activate(c)

    def part_copy(number, c):
        at = 3 * number + c
        return remote(
            part_out.at[number, chunk(c)], part_in.at[number, chunk(c)], part_send, part_recv.at[at], partner
        )

    finals = (value_grad, gate_grad, out_grad)
    scatters = [
        [Scatter(torus, g, color, grads, landed, sums, finals, send, recv) for color in range(3)]
        for g in range(GRADS)
    ]

    def weight_grad(g, rows_of, right, n):
        for m in range(4):
            term = dot(rows_of(m), right[:, 256 * n : 256 * n + 256], ((0,), (0,)))
            for half in range(2):
                grads[g, 2 * n + half, m // 2, 2 * (m % 2) : 2 * (m % 2) + 2] = (
                    term[:, 128 * half : 128 * half + 128].reshape(2, 4, 2, 24, 128).astype(BF16)
                )
        scatters[g][n].begin(0)

    def conv_slope(c):
        stat_copy(1, c).wait_recv()

        def body(first):
            rows = pl.ds(first, GROUP)
            mean, cross = get_stats(1, rows)
            scale = rstd2[rows, :]
            for j in range(6):
                slope = scale * (ds[rows, 128 * j : 128 * j + 128] - mean - cb[j, rows, :] * cross)
                db[j, pl.ds(pl.multiple_of(first + EDGE, GROUP), GROUP), :] = slope.astype(BF16).astype(F32)

        groups(c, body)

    conv_slope(0)
    conv_slope(2)
    d_halo = halo(db, 2)
    for copy in d_halo:
        copy.start()
    for n in range(3):
        weight_grad(2, lambda m: uf[m // 2, :, 384 * (m % 2) : 384 * (m % 2) + 384], sw, n)
    for color in range(3):
        scatters[2][color].straight()

    conv_slope(1)

    def tap_terms(j):
        def block(b, totals):
            first = pl.multiple_of(BLOCK * b, BLOCK)
            slopes = [near(db, j, pl.multiple_of(first + (EDGE + 8 * i), 8)) for i in range(BLOCK // 8)]
            totals = list(totals)
            for m in range(BLOCK - 8 + TAPS):
                shifted = near(hb, j, first + (EDGE - REACH + m))
                for i in range(BLOCK // 8):
                    if 0 <= m - 8 * i < TAPS:
                        totals[m - 8 * i] = totals[m - 8 * i] + shifted * slopes[i]
            return tuple(totals)

        zeros = tuple(jnp.zeros((8, 128), F32) for _ in range(TAPS))
        totals = lax.fori_loop(0, FRAMES // BLOCK, block, zeros)
        for k in range(TAPS):
            tap_acc[j, k, :] = jnp.sum(totals[k], 0)
        tap_acc[j, TAPS, :] = jnp.zeros((128,), F32)

    tap_sums = [TapSum(torus, color, slots, tap_send, tap_recv) for color in range(3)]

    def tap_color(color):
        tap_sums[color].begin(0, tap_acc[2 * color : 2 * color + 2])

    def straight(g):
        for color in range(3):
            scatters[g][color].straight()

    def relay(g, colors=(0, 1, 2)):
        for color in colors:
            scatters[g][color].relay()

    def finish(g, phase, colors=(0, 1, 2)):
        for color in colors:
            scatters[g][color].finish(phase)

    def tap_step(phase, color):
        total = tap_sums[color].finish(phase)
        if phase < 2:
            tap_sums[color].begin(phase + 1, total)
        else:
            for half in range(2):
                j = 2 * color + half
                taps_grad[:, 128 * j : 128 * j + 128] = total[half, 0:TAPS, :]

    def gate_slopes(c):
        def body(first):
            rows = pl.ds(first, GROUP)
            valid = valid_rows(first, GROUP)
            for j in range(6):
                columns = slice(128 * j, 128 * j + 128)
                sigma = sg[rows, columns]
                slope = cb[j, rows, :] * valid * sigma
                dv[rows, columns] = slope.astype(BF16)
                dg[rows, columns] = (slope * vb[rows, columns] * (1.0 - sigma)).astype(BF16)

        groups(c, body)

    convolve(db, 1, lambda k: TAPS - 1 - k, output_part)
    part_copy(0, 1).start()
    gate_slopes(1)
    halo_end(d_halo, db)
    convolve(db, 0, lambda k: TAPS - 1 - k, output_part)
    part_copy(0, 0).start()
    gate_slopes(0)
    relay(2)
    convolve(db, 2, lambda k: TAPS - 1 - k, output_part)
    part_copy(0, 2).start()
    gate_slopes(2)

    for n in range(3):
        weight_grad(0, lambda m: nb[:, 384 * m : 384 * m + 384], dv, n)
    for n in range(3):
        weight_grad(1, lambda m: nb[:, 384 * m : 384 * m + 384], dg, n)

    def features(c, n, half):
        rows = pl.ds(pl.multiple_of(half * HALF + 256 * n, 256), 256)
        return dot(dv[chunk(c), :], wv[rows, :], ((1,), (1,))) + dot(dg[chunk(c), :], wg[rows, :], ((1,), (1,)))

    def features_over(c):
        for n in range(3):
            part_out[1, chunk(c), 256 * n : 256 * n + 256] = features(c, n, other).astype(BF16)
        part_copy(1, c).start()

    def features_here(c):
        for n in range(3):
            vb[chunk(c), 256 * n : 256 * n + 256] = features(c, n, me)

    def output_rows(c):
        part_copy(0, c).wait_recv()

        def body(first):
            rows = pl.ds(first, GROUP)
            total = xf[me, rows, :].astype(F32) + (po[rows, :] + part_in[0, rows, :].astype(F32))
            xf[me, rows, :] = total.astype(BF16)

        groups(c, body)
        store = pltpu.make_async_copy(xf.at[me, chunk(c)], out.at[chunk(c)], store_sem.at[0])
        store.start()

    def feature_stats(c):
        part_copy(1, c).wait_recv()

        def body(first):
            rows = pl.ds(first, GROUP)
            slope = vb[rows, :] + part_in[1, rows, :].astype(F32)
            vb[rows, :] = slope
            unit = nb[rows, pl.ds(pl.multiple_of(me * HALF, HALF), HALF)].astype(F32)
            put_stats(2, rows, jnp.sum(slope, -1, keepdims=True), jnp.sum(slope * unit, -1, keepdims=True))

        groups(c, body)
        stat_copy(2, c).start()

    def input_rows(c):
        stat_copy(2, c).wait_recv()

        def body(first):
            rows = pl.ds(first, GROUP)
            mean, cross = get_stats(2, rows)
            scale = rstd1[rows, 0:1]
            unit = nb[rows, pl.ds(pl.multiple_of(me * HALF, HALF), HALF)].astype(F32)
            total = uf[me, rows, :].astype(F32) + scale * (vb[rows, :] - mean - unit * cross)
            uf[me, rows, :] = total.astype(BF16)

        groups(c, body)
        store = pltpu.make_async_copy(uf.at[me, chunk(c)], grad_in.at[chunk(c)], store_sem.at[1])
        store.start()

    straight(0)
    tap_terms(0)
    relay(0, (0,))
    tap_terms(1)
    tap_color(0)
    relay(0, (1, 2))
    straight(1)
    tap_terms(2)
    finish(2, 0)
    tap_terms(3)
    tap_color(1)
    relay(1, (0,))
    tap_terms(4)
    relay(1, (1, 2))
    tap_terms(5)
    tap_color(2)
    tap_step(0, 0)
    features_over(0)
    finish(0, 0, (0,))
    features_over(1)
    finish(0, 0, (1, 2))
    features_over(2)
    finish(1, 0, (0,))
    features_here(0)
    finish(1, 0, (1,))
    tap_step(0, 1)
    features_here(1)
    finish(1, 0, (2,))
    tap_step(0, 2)
    features_here(2)
    tap_step(1, 0)
    for c in range(CHUNKS):
        feature_stats(c)
    finish(0, 1, (0,))
    for c in range(CHUNKS):
        output_rows(c)
    finish(0, 1, (1, 2))
    finish(2, 1)
    for c in range(CHUNKS):
        input_rows(c)
    finish(1, 1, (0,))
    finish(1, 1, (1,))
    tap_step(1, 1)
    finish(1, 1, (2,))
    tap_step(1, 2)
    finish(0, 2)
    stores = [store_small(0)]
    tap_step(2, 0)
    finish(2, 2)
    stores.append(store_small(2))
    finish(1, 2)
    stores.append(store_small(1))
    tap_step(2, 1)
    tap_step(2, 2)
    stores.append(store_small(3))

    for color in range(3):
        for phase in range(3):
            wait_bytes(torus, landed[color][phase], send.at[color * 3 + phase], sent=True)
    wait_bytes(torus, slots.at[:, :, 0:3], tap_send, sent=True)
    wait_bytes(torus, xf.at[me], x_send, sent=True)
    wait_bytes(torus, uf.at[me], u_send, sent=True)
    wait_bytes(torus, hb.at[:, 0 : 4 * EDGE], halo_send, sent=True)
    wait_bytes(torus, stat_out, stat_send, sent=True)
    wait_bytes(torus, part_out, part_send, sent=True)
    pltpu.make_async_copy(xf.at[me], out, store_sem.at[0]).wait()
    pltpu.make_async_copy(uf.at[me], grad_in, store_sem.at[1]).wait()
    for store in stores:
        store.wait()


def place_kernel(*refs):
    sources, targets, held, (load, store) = refs[:6], refs[6:12], refs[12:18], refs[18:]
    parts = [(n, slice(None)) for n in range(2, 6)]
    parts += [(n, pl.ds(ROWS * c, ROWS)) for n in range(2) for c in range(CHUNKS)]
    pairs = [
        (
            pltpu.make_async_copy(sources[n].at[rows], held[n].at[rows], load.at[at]),
            pltpu.make_async_copy(held[n].at[rows], targets[n].at[rows], store.at[at]),
        )
        for at, (n, rows) in enumerate(parts)
    ]
    for first, _ in pairs:
        first.start()
    for first, second in pairs:
        first.wait()
        second.start()
    for _, second in pairs:
        second.wait()


def scratch_shapes():
    vmem, dma = pltpu.VMEM, pltpu.SemaphoreType.DMA
    shapes = [vmem((GRADS, 2, 3) + dims + (24, 128), BF16) for order in ORDERS for dims in LEFT[order]]
    shapes += [vmem((GRADS, 2) + dims + (24, 128), BF16) for order in ORDERS for dims in LEFT[order][:2]]
    shapes += [vmem((3, 3, 4, 2, 32, 128), BF16), dma((9,)), dma((GRADS * 3 * 4,)), dma(()), dma((9,))]
    square, padded = (FRAMES, HALF), (6, FRAMES + 2 * EDGE, 128)
    shapes += [
        vmem((GRADS, 6, 2, 4, 4, 2, 24, 128), BF16),
        vmem((2,) + square, BF16),
        vmem((2,) + square, BF16),
        vmem((WIDTH, HALF), BF16),
        vmem((WIDTH, HALF), BF16),
        vmem((2,) + square, BF16),
        vmem((FRAMES, WIDTH), BF16),
        vmem((FRAMES, 128), F32),
        vmem(square, F32),
        vmem(square, F32),
        vmem(padded, F32),
        vmem(padded, F32),
        vmem((6, FRAMES, 128), F32),
        vmem(square, BF16),
        vmem(square, F32),
        vmem((FRAMES, 128), F32),
        vmem((3, FRAMES, 128), F32),
        vmem((3, FRAMES, 128), F32),
        vmem(square, BF16),
        vmem(square, BF16),
        vmem(square, F32),
        vmem((2,) + square, BF16),
        vmem((2,) + square, BF16),
        vmem((TAPS, HALF), BF16),
        vmem((1, 1), jnp.int32),
        vmem((6, TAPS, 8, 128), F32),
        vmem((6, TAPS + 1, 128), F32),
        vmem((24, HALF), F32), vmem((24, HALF), F32), vmem((24, HALF), F32), vmem((TAPS, HALF), F32),
        dma((10,)), dma(()), dma((3,)), dma(()), dma(()), dma(()), dma((4,)),
        dma(()), dma((9,)), dma(()), dma((6,)), dma((6,)),
    ]
    return shapes


def shards(inputs, lengths, cotangent, w_value, w_gate, kernel_taps, w_out):
    here = pl.BlockSpec(memory_space=pl.ANY)
    rows = jax.ShapeDtypeStruct((FRAMES, HALF), BF16)
    block = jax.ShapeDtypeStruct((24, HALF), F32)
    results = (rows, rows, block, block, jax.ShapeDtypeStruct((TAPS, HALF), F32), block)
    output, input_gradient, value_grad, gate_grad, kernel_grad, out_grad = pl.pallas_call(
        kernel,
        out_shape=results,
        in_specs=[here] * 7,
        out_specs=(here,) * 6,
        scratch_shapes=scratch_shapes(),
        compiler_params=pltpu.CompilerParams(
            collective_id=0, has_side_effects=True, vmem_limit_bytes=67043328
        ),
    )(lengths.reshape(1, 1), inputs[0], cotangent[0], w_value, w_gate, kernel_taps, w_out)
    output, input_gradient, value_grad, gate_grad, kernel_grad, out_grad = pl.pallas_call(
        place_kernel,
        out_shape=results,
        in_specs=[here] * 6,
        out_specs=(here,) * 6,
        scratch_shapes=[pltpu.VMEM(result.shape, result.dtype) for result in results]
        + [pltpu.SemaphoreType.DMA((10,)), pltpu.SemaphoreType.DMA((10,))],
    )(output, input_gradient, value_grad, gate_grad, kernel_grad, out_grad)
    return (output[None], input_gradient[None], value_grad, gate_grad, kernel_grad, out_grad.T)


def solution(mesh):
    return jax.shard_map(
        shards,
        mesh=mesh,
        in_specs=(
            P("dp", "seq", "tensor"),
            P("dp"),
            P("dp", "seq", "tensor"),
            P(None, "tensor"),
            P(None, "tensor"),
            P(None, "tensor"),
            P("tensor", None),
        ),
        out_specs=(
            P("dp", "seq", "tensor"),
            P("dp", "seq", "tensor"),
            P(("seq", "dp"), "tensor"),
            P(("seq", "dp"), "tensor"),
            P(None, "tensor"),
            P("tensor", ("seq", "dp")),
        ),
        check_vma=False,
    )
```
